256 devices in a mesh: depth: 32 (over y, z_lo, core), sample: 4 (over x), filter: 2 (over z_hi).
Axes of the slice: x: 4, y: 4, z: 8 (z_hi: 2, z_lo: 4; z = z_hi * 4 + z_lo), core: 2. Of those that a mesh axis runs over, the one named last changes fastest.
Arguments:
- inputs: float32 [4, 64, 8, 8, 256], P('sample', 'depth', None, None, 'filter'), may hold values from -6 to 6
- pre_gelu: float32 [4, 64, 8, 8, 256], P('sample', 'depth', None, None, 'filter'), may hold values from -6 to 6
- output_grad: float32 [4, 64, 8, 8, 256], P('sample', 'depth', None, None, 'filter'), may hold values from -6 to 6
- first_weight: float32 [27, 256, 256], P(None, None, 'filter'), may hold values from -0.078125 to 0.078125
- second_weight: float32 [27, 256, 256], P(None, None, 'filter'), may hold values from -0.078125 to 0.078125
Outputs:
- input_grad: float32 [4, 64, 8, 8, 256], P('sample', 'depth', None, None, 'filter')
- first_weight_grad: float32 [27, 256, 256], P(None, 'depth', 'filter')
- second_weight_grad: float32 [27, 256, 256], P(None, 'depth', 'filter')
The draws below stay inside these ranges and needn't reach their ends.
All inputs are finite; a program needn't handle non-finite values.
Results may differ from the reference program's by a relative error of at most 0.000098.
Values sent between devices are 32-bit elements; how exact they have to be, the bound alone decides.
A program may use at most 64 MiB of HBM per device.

```python
import math
import jax
import jax.numpy as jnp
from jax import lax

C = 256
GRID_H = 8
GRID_W = 8
SAMPLES = 4
NDEPTH = 64


def with_spikes(result, own_key, source, target, shards_of, factor):
    owner, partner = [(jnp.arange(result.shape[position]) // (result.shape[position] // shards_of)).reshape([-1 if axis == position else 1 for axis in range(result.ndim)]) for position in (source, target)]
    chosen = jax.random.permutation(own_key, shards_of)[partner]
    strong = (owner == chosen) | (owner == (partner + shards_of // 2) % shards_of)
    return jnp.where(strong, factor * result, result)


def steps_of(stream_key, extent, shards, low, high):
    loudness = 1.0
    for position, parts in shards:
        steps = jax.random.uniform(jax.random.fold_in(jax.random.fold_in(stream_key, 6), position), (parts,), jnp.float32, low / len(shards), high / len(shards))
        loudness = loudness * jnp.repeat(jnp.exp(steps), extent[position] // parts).reshape((-1,) + (1,) * (len(extent) - 1 - position))
    return loudness


def scatter_about(rng, extent, deviation, bound, shards=(), kind=jnp.bfloat16):
    result = jax.random.normal(rng, extent, jnp.float32) * deviation
    if len(shards) > 0:
        result = steps_of(rng, extent, shards, -0.22, 0.18) * result
    return jnp.clip(result, min=-bound, max=bound).astype(kind)


def noise_with(stream_key, dims, deviation, bound, pieces, heavy, kind=jnp.bfloat16):
    result = deviation * jax.random.normal(stream_key, dims, jnp.float32)
    if pieces:
        result = result * steps_of(stream_key, dims, pieces, -0.22, 0.18)
    return jnp.clip(with_spikes(result, jax.random.fold_in(stream_key, 3), *heavy), -bound, bound).astype(kind)


def setup_inputs(seed: int = 0) -> dict:
    seeds = jax.random.split(jax.random.key(seed), 6)
    return {
        "inputs": noise_with(seeds[0], (SAMPLES, NDEPTH, GRID_H, GRID_W, C), 1.0, 6.0, ((0, 4), (1, 32), (4, 2)), (1, 4, 32, 2.75), jnp.float32),
        "pre_gelu": noise_with(seeds[1], (SAMPLES, NDEPTH, GRID_H, GRID_W, C), 1.0, 6.0, ((0, 4), (1, 32), (4, 2)), (1, 4, 32, 2.75), jnp.float32),
        "output_grad": scatter_about(seeds[2], (SAMPLES, NDEPTH, GRID_H, GRID_W, C), 1.0, 6.0, ((0, 4), (1, 32), (4, 2)), jnp.float32),
        "first_weight": scatter_about(seeds[3], (27, C, C), (27 * C) ** -0.5, 0.078125, ((2, 2),), jnp.float32),
        "second_weight": scatter_about(seeds[4], (27, C, C), (27 * C) ** -0.5, 0.078125, ((2, 2),), jnp.float32),
    }


def gelu_pair(pre):
    normal_cdf = 0.5 * (1.0 + lax.erf(pre * 0.7071067811865476))
    density = jnp.exp(-0.5 * pre * pre) * 0.3989422804014327
    return (pre * normal_cdf, normal_cdf + pre * density)

def conv_same(field, kernel_flat):
    kernel = kernel_flat.reshape(3, 3, 3, kernel_flat.shape[1], kernel_flat.shape[2])
    return lax.conv_general_dilated(field, kernel, (1, 1, 1), ((1, 1), (1, 1), (1, 1)), dimension_numbers=('NDHWC', 'DHWIO', 'NDHWC'), precision=lax.Precision.HIGHEST)

def reference(inputs, pre_gelu, output_grad, first_weight, second_weight):
    activated, slope = gelu_pair(pre_gelu)
    unused_second, second_back = jax.vjp(conv_same, activated, second_weight)
    act_grad, second_raw = second_back(output_grad)
    pre_grad = act_grad * slope
    unused_first, first_back = jax.vjp(conv_same, inputs, first_weight)
    input_grad, first_raw = first_back(pre_grad)
    cells = inputs.shape[0] * inputs.shape[1] * inputs.shape[2] * inputs.shape[3]
    factor = 1.0 / math.sqrt(cells)
    return (input_grad, first_raw * factor, second_raw * factor)
```

```python
import jax
import jax.numpy as jnp
from jax import lax
from jax.experimental import pallas as pl
from jax.experimental.pallas import tpu as pltpu
from jax.sharding import PartitionSpec as P

F32 = jnp.float32
BF16 = jnp.bfloat16
TAPS = 27
ROWS = TAPS * 8
K_CONV = TAPS * 128
THIRD = 9 * 128


def remote(src, dst, send, recv, device):
    return pltpu.make_async_remote_copy(
        src_ref=src,
        dst_ref=dst,
        send_sem=send,
        recv_sem=recv,
        device_id=device,
        device_id_type=pl.DeviceIdType.MESH,
    )


def gelu_pair(pre):
    normal_cdf = 0.5 * (1.0 + lax.erf(pre * 0.7071067811865476))
    density = jnp.exp(-0.5 * pre * pre) * 0.3989422804014327
    return pre * normal_cdf, normal_cdf + pre * density


def parts_of(value):
    high = value.astype(BF16)
    return high, (value - high.astype(F32)).astype(BF16)


def lanes_of(rows):
    return lax.broadcasted_iota(jnp.int32, (rows, 128), 1)


def moved(base, dh, dw):
    if dh == 0 and dw == 0:
        return base
    lane = lanes_of(base.shape[0])
    h = (lane // 8) % 8 + dh
    w = lane % 8 + dw
    inside = (h >= 0) & (h < 8) & (w >= 0) & (w < 8)
    return jnp.where(inside, pltpu.roll(base, (-(dh * 8 + dw)) % 128, 1), 0.0)


def kernel(
    inp_hbm, pre_hbm, og_hbm, w1_hbm, w2_hbm,
    grad_out, first_out, second_out,
    og_v, pre_v, inp_v, wf, wb1, wb2, cols, acc,
    og_halo, pg_halo, pair_pre, pair_inp, slope_v, field_t, slices, owned, low_act, high_act,
    og_all, pg_all, rhs, lhs, part_out, part_in, pgt_v, pg_v,
    y_out, y_in, y_sum, z_out, z_in, x_all, x_out,
    load_sem, halo_s, halo_r, pair_s, pair_r, ring_s, ring_r, slice_s, slice_r, edge_s, edge_r,
    y_s, y_r, z_s, z_r, x_s, x_r,
):
    d = lax.axis_index("depth")
    s = lax.axis_index("sample")
    f = lax.axis_index("filter")
    c = d % 2
    chip = d // 2
    zl = chip % 4
    y = d // 8
    partner = d + 1 - 2 * c

    to_filter = (d, s, 1 - f)
    group = [(0, 1)] + [(k, o) for k in (2, 1, 3) for o in (0, 1)]

    def group_device(k, o):
        return (partner if o else d, (s + k) % 4, f)

    to_next, to_last = ((d + 1) % 32, s, f), ((d + 31) % 32, s, f)
    to_next_chip, to_last_chip = ((d + 2) % 32, s, f), ((d + 30) % 32, s, f)

    def to_y(k):
        return ((d + 8 * k) % 32, s, f)

    def to_z(k):
        return (y * 8 + ((zl + k) % 4) * 2 + c, s, f)

    loads = [
        pltpu.make_async_copy(og_hbm, og_v, load_sem.at[0]),
        pltpu.make_async_copy(pre_hbm, pre_v, load_sem.at[1]),
        pltpu.make_async_copy(inp_hbm, inp_v, load_sem.at[2]),
        pltpu.make_async_copy(w2_hbm, wf.at[0], load_sem.at[3]),
        pltpu.make_async_copy(w1_hbm, wf.at[1], load_sem.at[4]),
    ]
    for load in loads:
        load.start()

    barrier = pltpu.get_barrier_semaphore()
    friends = [to_filter, to_next, to_last, to_next_chip, to_last_chip]
    friends += [group_device(k, o) for k, o in group]
    friends += [to_y(k) for k in (1, 2, 3)] + [to_z(k) for k in (1, 2, 3)]
    for friend in friends:
        pl.semaphore_signal(barrier, inc=1, device_id=friend, device_id_type=pl.DeviceIdType.MESH)

    started = []

    def send(*args):
        copy = remote(*args)
        copy.start()
        started.append(copy)
        return copy

    lane = lanes_of(128)
    left = lane < 64

    def patch(base, depth_tap):
        for b in range(3):
            for e in range(3):
                t = 9 * depth_tap + 3 * b + e
                high, low = parts_of(moved(base, 1 - b, 1 - e))
                cols[t * 128 : (t + 1) * 128, 0:128] = high
                cols[t * 128 : (t + 1) * 128, 128:256] = low

    def patch_edges(own, halo_ref):
        edge = halo_ref[...].T
        edge = jnp.where(left & (d == 0), 0.0, edge)
        edge = jnp.where((~left) & (d == 31), 0.0, edge)
        swapped = pltpu.roll(own, 64, 1)
        patch(jnp.where(left, swapped, edge), 0)
        patch(jnp.where(left, edge, swapped), 2)

    def split_weight(n, wb):
        def body(t, carry):
            at = pl.ds(pl.multiple_of(t * 128, 128), 128)
            for h in range(2):
                high, low = parts_of(wf[n, t, h * 128 : (h + 1) * 128, :])
                wb[h, 0:128, at] = high
                wb[h, 128:256, at] = low
            return carry

        lax.fori_loop(0, TAPS, body, 0)

    def product(wb, h, third):
        at = slice(third * THIRD, (third + 1) * THIRD)
        return jnp.dot(wb[h, :, at], cols[at, :], preferred_element_type=F32)

    def fold(total):
        return (total[0:128, 0:128] + total[0:128, 128:256]) + (
            total[128:256, 0:128] + total[128:256, 128:256]
        )

    def conv_middle(wb):
        for h in range(2):
            acc[h] = product(wb, h, 1)

    def conv_rest(wb, h):
        return fold(acc[h] + (product(wb, h, 0) + product(wb, h, 2)))

    loads[0].wait()
    og_t = og_v[...].T
    patch(og_t, 1)
    og_all[c, 0] = og_v[...]
    loads[1].wait()
    act_t, slope_t = gelu_pair(pre_v[...].T)
    slope_v[...] = slope_t
    field_t[0, f] = act_t
    loads[2].wait()
    field_t[1, f] = inp_v[...].T

    pl.semaphore_wait(barrier, len(friends))

    og_edges = [
        send(og_v.at[pl.ds(64, 64)], og_halo.at[pl.ds(0, 64)], halo_s.at[0], halo_r.at[0], to_next),
        send(og_v.at[pl.ds(0, 64)], og_halo.at[pl.ds(64, 64)], halo_s.at[1], halo_r.at[1], to_last),
    ]
    pairs = [
        send(pre_v, pair_pre, pair_s.at[0], pair_r.at[0], to_filter),
        send(inp_v, pair_inp, pair_s.at[1], pair_r.at[1], to_filter),
    ]

    def gather(src, dst, n):
        return [
            send(src, dst.at[c, (4 - k) % 4], ring_s.at[n, i], ring_r.at[n, i], group_device(k, o))
            for i, (k, o) in enumerate(group)
        ]

    og_gather = gather(og_v, og_all, 0)

    loads[3].wait()
    split_weight(0, wb2)
    conv_middle(wb2)
    loads[4].wait()
    split_weight(1, wb1)

    for copy in og_edges:
        copy.wait_recv()
    patch_edges(og_t, og_halo)
    part_out[0] = conv_rest(wb2, 1 - f)
    act_pair = send(part_out.at[0], part_in.at[0], pair_s.at[2], pair_r.at[2], to_filter)
    own_part = conv_rest(wb2, f)

    sliced = []
    for n, recv in ((0, pair_pre), (1, pair_inp)):
        pairs[n].wait_recv()
        other = recv[...].T
        if n == 0:
            other, _ = gelu_pair(other)
        field_t[n, 1 - f] = other
        for half in range(2):
            for core in range(2):
                for x in range(4):
                    for hi in range(2):
                        for e in range(2):
                            row = hi * 8 + e * 4
                            slices[n, core, x, half, row : row + 4, :] = field_t[
                                n, half, pl.ds(64 * hi + 8 * core + 2 * x + e, 4, stride=16), :
                            ]
        owned[n, c, 0] = slices[n, c, s]
        sliced.append(
            [
                send(
                    slices.at[n, (1 - c) if o else c, (s + k) % 4],
                    owned.at[n, c, (4 - k) % 4],
                    slice_s.at[n, i],
                    slice_r.at[n, i],
                    group_device(k, o),
                )
                for i, (k, o) in enumerate(group)
            ]
        )
    edges = []
    for n in range(2):
        for copy in sliced[n]:
            copy.wait_recv()
        edges.append(
            [
                send(owned.at[n, 1], low_act.at[n], edge_s.at[n, 0], edge_r.at[n, 0], to_next_chip),
                send(owned.at[n, 0], high_act.at[n], edge_s.at[n, 1], edge_r.at[n, 1], to_last_chip),
            ]
        )

    act_pair.wait_recv()
    pg_t = (own_part + part_in[0]) * slope_v[...]
    pgt_v[...] = pg_t
    pg_v[...] = pg_t.T
    pg_gather = gather(pg_v, pg_all, 1)
    pg_edges = [
        send(pg_v.at[pl.ds(64, 64)], pg_halo.at[pl.ds(0, 64)], halo_s.at[2], halo_r.at[2], to_next),
        send(pg_v.at[pl.ds(0, 64)], pg_halo.at[pl.ds(64, 64)], halo_s.at[3], halo_r.at[3], to_last),
    ]
    pg_all[c, 0] = pg_v[...]
    patch(pg_t, 1)
    conv_middle(wb1)

    def make_rhs(n, ref):
        high, low = parts_of(ref[...].reshape(1024, 128))
        rhs[n, :, 0:128] = high
        rhs[n, :, 128:256] = low

    def make_lhs(n):
        for copy in edges[n]:
            copy.wait_recv()
        near = lanes_of(32) < 64

        def body(k, carry):
            first = owned[n, 0, k].reshape(32, 128)
            last = owned[n, 1, k].reshape(32, 128)
            below = jnp.where(chip == 0, 0.0, low_act[n, k].reshape(32, 128))
            above = jnp.where(chip == 15, 0.0, high_act[n, k].reshape(32, 128))

            def joined(one, two):
                return pltpu.roll(jnp.where(near, two, one), 64, 1)

            middle = joined(first, last)
            bases = [
                (joined(below, first), ((0, 0),)),
                (first, ((1, 0),)),
                (middle, ((2, 0), (0, 1))),
                (last, ((1, 1),)),
                (joined(last, above), ((2, 1),)),
            ]
            for base, uses in bases:
                for b in range(3):
                    for e in range(3):
                        value = moved(base, b - 1, e - 1)
                        high = value.astype(BF16).astype(F32)
                        low = value - high
                        for yy in range(4):
                            rows = slice(yy * 8, yy * 8 + 8)
                            tile = jnp.concatenate([high[rows], low[rows]], axis=0).astype(BF16)
                            for a, core in uses:
                                t = 9 * a + 3 * b + e
                                at = pl.ds(pl.multiple_of(core * 512 + k * 128, 128), 128)
                                lhs[n, yy, t * 16 : (t + 1) * 16, at] = tile
            return carry

        lax.fori_loop(0, 4, body, 0)

    def raw_chunk(n, k):
        total = jnp.dot(lhs[n, (y + k) % 4], rhs[n], preferred_element_type=F32)
        total = (total[:, 0:128] + total[:, 128:256]).reshape(TAPS, 16, 128)
        return (total[:, 0:8] + total[:, 8:16]).reshape(ROWS, 128)

    def raw(n):
        copies = []
        for k in (2, 1, 3):
            y_out[n, k] = raw_chunk(n, k)
            copies.append(
                send(y_out.at[n, k], y_in.at[n, 4 - k], y_s.at[n, k], y_r.at[n, k], to_y(k))
            )
        y_sum[n] = raw_chunk(n, 0)
        return copies

    for copy in og_gather:
        copy.wait_recv()
    make_rhs(0, og_all)
    make_lhs(0)
    second_y = raw(0)
    make_lhs(1)
    for copy in pg_gather:
        copy.wait_recv()
    make_rhs(1, pg_all)
    first_y = raw(1)

    for copy in pg_edges:
        copy.wait_recv()
    patch_edges(pgt_v[...], pg_halo)
    part_out[1] = conv_rest(wb1, 1 - f)
    in_pair = send(part_out.at[1], part_in.at[1], pair_s.at[3], pair_r.at[3], to_filter)
    own_grad = conv_rest(wb1, f)

    for n, copies in ((0, second_y), (1, first_y)):
        for copy in copies:
            copy.wait_recv()
        y_sum[n] = (y_sum[n] + y_in[n, 1]) + (y_in[n, 2] + y_in[n, 3])
        for zz in range(4):
            z_out[zz, n, 0:54, :] = y_sum[n, pl.ds(zz, 54, stride=4), :]
            z_out[zz, n, 54:56, :] = jnp.zeros((2, 128), F32)
    z_copies = [
        send(z_out.at[(zl + k) % 4], z_in.at[4 - k], z_s.at[k], z_r.at[k], to_z(k)) for k in (1, 2, 3)
    ]
    for copy in z_copies:
        copy.wait_recv()
    x_out[...] = ((z_out[zl] + z_in[1]) + (z_in[2] + z_in[3])) * (1.0 / 128.0)
    x_copies = [
        send(x_out, x_all.at[s], x_s.at[k], x_r.at[k], (d, (s + k) % 4, f)) for k in (1, 2, 3)
    ]
    x_all[s] = x_out[...]

    in_pair.wait_recv()
    grad_out[...] = (own_grad + part_in[1]).T

    for copy in x_copies:
        copy.wait_recv()
    for n, out in ((0, second_out), (1, first_out)):
        for x in range(4):
            for e in range(2):
                out[pl.ds(2 * x + e, TAPS, stride=8), :] = x_all[x, n, pl.ds(e, TAPS, stride=2), :]

    for copy in started:
        copy.wait_send()


def local(inputs, pre_gelu, output_grad, first_weight, second_weight):
    shape = inputs.shape
    hbm = pl.BlockSpec(memory_space=pl.ANY)
    vmem = pl.BlockSpec(memory_space=pltpu.VMEM)
    dma = pltpu.SemaphoreType.DMA
    block = (128, 128)
    grad, first, second = pl.pallas_call(
        kernel,
        out_shape=(
            jax.ShapeDtypeStruct(block, F32),
            jax.ShapeDtypeStruct((ROWS, 128), F32),
            jax.ShapeDtypeStruct((ROWS, 128), F32),
        ),
        in_specs=[hbm] * 5,
        out_specs=(vmem, vmem, vmem),
        scratch_shapes=[
            pltpu.VMEM(block, F32),
            pltpu.VMEM(block, F32),
            pltpu.VMEM(block, F32),
            pltpu.VMEM((2, TAPS, 256, 128), F32),
            pltpu.VMEM((2, 256, K_CONV), BF16),
            pltpu.VMEM((2, 256, K_CONV), BF16),
            pltpu.VMEM((K_CONV, 256), BF16),
            pltpu.VMEM((2, 256, 256), F32),
            pltpu.VMEM(block, F32),
            pltpu.VMEM(block, F32),
            pltpu.VMEM(block, F32),
            pltpu.VMEM(block, F32),
            pltpu.VMEM(block, F32),
            pltpu.VMEM((2, 2) + block, F32),
            pltpu.VMEM((2, 2, 4, 2, 16, 128), F32),
            pltpu.VMEM((2, 2, 4, 2, 16, 128), F32),
            pltpu.VMEM((2, 4, 2, 16, 128), F32),
            pltpu.VMEM((2, 4, 2, 16, 128), F32),
            pltpu.VMEM((2, 4) + block, F32),
            pltpu.VMEM((2, 4) + block, F32),
            pltpu.VMEM((2, 1024, 256), BF16),
            pltpu.VMEM((2, 4, TAPS * 16, 1024), BF16),
            pltpu.VMEM((2,) + block, F32),
            pltpu.VMEM((2,) + block, F32),
            pltpu.VMEM(block, F32),
            pltpu.VMEM(block, F32),
            pltpu.VMEM((2, 4, ROWS, 128), F32),
            pltpu.VMEM((2, 4, ROWS, 128), F32),
            pltpu.VMEM((2, ROWS, 128), F32),
            pltpu.VMEM((4, 2, 56, 128), F32),
            pltpu.VMEM((4, 2, 56, 128), F32),
            pltpu.VMEM((4, 2, 56, 128), F32),
            pltpu.VMEM((2, 56, 128), F32),
            dma((5,)),
            dma((4,)), dma((4,)),
            dma((4,)), dma((4,)),
            dma((2, 7)), dma((2, 7)),
            dma((2, 7)), dma((2, 7)),
            dma((2, 2)), dma((2, 2)),
            dma((2, 4)), dma((2, 4)),
            dma((4,)), dma((4,)),
            dma((4,)), dma((4,)),
        ],
        compiler_params=pltpu.CompilerParams(
            collective_id=1, has_side_effects=True, vmem_limit_bytes=56 << 20
        ),
        name="backward",
    )(
        inputs.reshape(block),
        pre_gelu.reshape(block),
        output_grad.reshape(block),
        first_weight,
        second_weight,
    )
    return grad.reshape(shape), first.reshape(TAPS, 8, 128), second.reshape(TAPS, 8, 128)


def solution(mesh):
    field = P("sample", "depth", None, None, "filter")
    return jax.shard_map(
        local,
        mesh=mesh,
        in_specs=(field, field, field, P(None, None, "filter"), P(None, None, "filter")),
        out_specs=(field, P(None, "depth", "filter"), P(None, "depth", "filter")),
        check_vma=False,
    )
```

```python
import jax
import jax.numpy as jnp
from jax import lax
from jax.experimental import pallas as pl
from jax.experimental.pallas import tpu as pltpu
from jax.sharding import PartitionSpec as P

F32 = jnp.float32
BF16 = jnp.bfloat16
TAPS = 27
ROWS = TAPS * 8
K_CONV = TAPS * 128
THIRD = 9 * 128


def remote(src, dst, send, recv, device):
    return pltpu.make_async_remote_copy(
        src_ref=src,
        dst_ref=dst,
        send_sem=send,
        recv_sem=recv,
        device_id=device,
        device_id_type=pl.DeviceIdType.MESH,
    )


def gelu_pair(pre):
    normal_cdf = 0.5 * (1.0 + lax.erf(pre * 0.7071067811865476))
    density = jnp.exp(-0.5 * pre * pre) * 0.3989422804014327
    return pre * normal_cdf, normal_cdf + pre * density


def parts_of(value):
    high = value.astype(BF16)
    return high, (value - high.astype(F32)).astype(BF16)


def lanes_of(rows):
    return lax.broadcasted_iota(jnp.int32, (rows, 128), 1)


def moved(base, dh, dw):
    if dh == 0 and dw == 0:
        return base
    lane = lanes_of(base.shape[0])
    h = (lane // 8) % 8 + dh
    w = lane % 8 + dw
    inside = (h >= 0) & (h < 8) & (w >= 0) & (w < 8)
    return jnp.where(inside, pltpu.roll(base, (-(dh * 8 + dw)) % 128, 1), 0.0)


def kernel(
    inp_hbm, pre_hbm, og_hbm, w1_hbm, w2_hbm,
    grad_out, x_all,
    og_v, pre_v, inp_v, wf, wb1, wb2, cols, acc,
    og_halo, pg_halo, slope_v, field_t, slices, owned, low_act, high_act,
    og_all, pg_all, rhs, lhs, part_out, part_in, pgt_v, pg_v,
    y_out, y_in, y_sum, z_out, z_in, x_out,
    load_sem, halo_s, halo_r, pair_s, pair_r, ring_s, ring_r, slice_s, slice_r, edge_s, edge_r,
    y_s, y_r, z_s, z_r, x_s, x_r,
):
    d = lax.axis_index("depth")
    s = lax.axis_index("sample")
    f = lax.axis_index("filter")
    c = d % 2
    chip = d // 2
    zl = chip % 4
    y = d // 8
    partner = d + 1 - 2 * c

    to_filter = (d, s, 1 - f)
    group = [(0, 1)] + [(k, o) for k in (2, 1, 3) for o in (0, 1)]
    wide = [(k, o, 1) for k in (2, 1, 3, 0) for o in (0, 1)] + [(k, o, 0) for k, o in group]

    def group_device(k, o, g=0):
        return (partner if o else d, (s + k) % 4, (1 - f) if g else f)

    to_next, to_last = ((d + 1) % 32, s, f), ((d + 31) % 32, s, f)
    to_next_chip, to_last_chip = ((d + 2) % 32, s, f), ((d + 30) % 32, s, f)

    def to_y(k):
        return ((d + 8 * k) % 32, s, f)

    def to_z(k):
        return (y * 8 + ((zl + k) % 4) * 2 + c, s, f)

    loads = [
        pltpu.make_async_copy(og_hbm, og_v, load_sem.at[0]),
        pltpu.make_async_copy(pre_hbm, pre_v, load_sem.at[1]),
        pltpu.make_async_copy(inp_hbm, inp_v, load_sem.at[2]),
        pltpu.make_async_copy(w2_hbm, wf.at[0], load_sem.at[3]),
        pltpu.make_async_copy(w1_hbm, wf.at[1], load_sem.at[4]),
    ]
    for load in loads:
        load.start()

    barrier = pltpu.get_barrier_semaphore()
    friends = [to_next, to_last, to_next_chip, to_last_chip]
    friends += [group_device(*step) for step in wide]
    friends += [to_y(k) for k in (1, 2, 3)] + [to_z(k) for k in (1, 2, 3)]
    for friend in friends:
        pl.semaphore_signal(barrier, inc=1, device_id=friend, device_id_type=pl.DeviceIdType.MESH)

    started = []

    def send(*args):
        copy = remote(*args)
        copy.start()
        started.append(copy)
        return copy

    lane = lanes_of(128)
    left = lane < 64

    def patch(base, depth_tap):
        for b in range(3):
            for e in range(3):
                t = 9 * depth_tap + 3 * b + e
                high, low = parts_of(moved(base, 1 - b, 1 - e))
                cols[t * 128 : (t + 1) * 128, 0:128] = high
                cols[t * 128 : (t + 1) * 128, 128:256] = low

    def patch_edges(own, halo_ref):
        edge = halo_ref[...].T
        edge = jnp.where(left & (d == 0), 0.0, edge)
        edge = jnp.where((~left) & (d == 31), 0.0, edge)
        swapped = pltpu.roll(own, 64, 1)
        patch(jnp.where(left, swapped, edge), 0)
        patch(jnp.where(left, edge, swapped), 2)

    def split_weight(n, wb):
        def body(t, carry):
            at = pl.ds(pl.multiple_of(t * 128, 128), 128)
            for h in range(2):
                high, low = parts_of(wf[n, t, h * 128 : (h + 1) * 128, :])
                wb[h, 0:128, at] = high
                wb[h, 128:256, at] = low
            return carry

        lax.fori_loop(0, TAPS, body, 0)

    def product(wb, h, third):
        at = slice(third * THIRD, (third + 1) * THIRD)
        return jnp.dot(wb[h, :, at], cols[at, :], preferred_element_type=F32)

    def fold(total):
        return (total[0:128, 0:128] + total[0:128, 128:256]) + (
            total[128:256, 0:128] + total[128:256, 128:256]
        )

    def conv_middle(wb):
        for h in range(2):
            acc[h] = product(wb, h, 1)

    def conv_rest(wb, h):
        return fold(acc[h] + (product(wb, h, 0) + product(wb, h, 2)))

    loads[1].wait()
    act_t, slope_t = gelu_pair(pre_v[...].T)
    slope_v[...] = slope_t
    field_t[0] = act_t
    loads[2].wait()
    field_t[1] = inp_v[...].T
    for n in range(2):
        for core in range(2):
            for x in range(4):
                for hi in range(2):
                    for e in range(2):
                        row = hi * 8 + e * 4
                        slices[core, x, n, row : row + 4, :] = field_t[
                            n, pl.ds(64 * hi + 8 * core + 2 * x + e, 4, stride=16), :
                        ]
    owned[c, 0, f] = slices[c, s]
    loads[0].wait()
    og_t = og_v[...].T
    og_all[c, 0] = og_v[...]

    pl.semaphore_wait(barrier, len(friends))

    og_edges = [
        send(og_v.at[pl.ds(64, 64)], og_halo.at[pl.ds(0, 64)], halo_s.at[0], halo_r.at[0], to_next),
        send(og_v.at[pl.ds(0, 64)], og_halo.at[pl.ds(64, 64)], halo_s.at[1], halo_r.at[1], to_last),
    ]
    sliced = [
        send(
            slices.at[(1 - c) if o else c, (s + k) % 4],
            owned.at[c, (4 - k) % 4, f],
            slice_s.at[i],
            slice_r.at[i],
            group_device(k, o, g),
        )
        for i, (k, o, g) in enumerate(wide)
    ]

    def gather(src, dst, n):
        return [
            send(src, dst.at[c, (4 - k) % 4], ring_s.at[n, i], ring_r.at[n, i], group_device(k, o))
            for i, (k, o) in enumerate(group)
        ]

    og_gather = gather(og_v, og_all, 0)

    patch(og_t, 1)
    loads[3].wait()
    split_weight(0, wb2)
    conv_middle(wb2)

    for copy in og_edges:
        copy.wait_recv()
    patch_edges(og_t, og_halo)
    part_out[0] = conv_rest(wb2, 1 - f)
    act_pair = send(part_out.at[0], part_in.at[0], pair_s.at[0], pair_r.at[0], to_filter)
    own_part = conv_rest(wb2, f)

    for copy in sliced:
        copy.wait_recv()
    edges = [
        send(owned.at[1], low_act, edge_s.at[0], edge_r.at[0], to_next_chip),
        send(owned.at[0], high_act, edge_s.at[1], edge_r.at[1], to_last_chip),
    ]

    def make_rhs(n, ref):
        high, low = parts_of(ref[...].reshape(1024, 128))
        rhs[n, :, 0:128] = high
        rhs[n, :, 128:256] = low

    def make_lhs(n, own_planes):
        near = lanes_of(32) < 64

        def joined(one, two):
            return pltpu.roll(jnp.where(near, two, one), 64, 1)

        def body(k, carry):
            first = owned[0, k, :, n].reshape(32, 128)
            last = owned[1, k, :, n].reshape(32, 128)
            if own_planes:
                bases = [
                    (first, ((1, 0),)),
                    (joined(first, last), ((2, 0), (0, 1))),
                    (last, ((1, 1),)),
                ]
            else:
                below = jnp.where(chip == 0, 0.0, low_act[k, :, n].reshape(32, 128))
                above = jnp.where(chip == 15, 0.0, high_act[k, :, n].reshape(32, 128))
                bases = [(joined(below, first), ((0, 0),)), (joined(last, above), ((2, 1),))]
            for base, uses in bases:
                for b in range(3):
                    for e in range(3):
                        value = moved(base, b - 1, e - 1)
                        high = value.astype(BF16).astype(F32)
                        low = value - high
                        for yy in range(4):
                            rows = slice(yy * 8, yy * 8 + 8)
                            tile = jnp.concatenate([high[rows], low[rows]], axis=0).astype(BF16)
                            for a, core in uses:
                                t = 9 * a + 3 * b + e
                                at = pl.ds(pl.multiple_of(core * 512 + k * 128, 128), 128)
                                lhs[n, yy, t * 16 : (t + 1) * 16, at] = tile
            return carry

        lax.fori_loop(0, 4, body, 0)

    def raw_chunk(n, k):
        total = jnp.dot(lhs[n, (y + k) % 4], rhs[n], preferred_element_type=F32)
        total = (total[:, 0:128] + total[:, 128:256]).reshape(TAPS, 16, 128)
        return (total[:, 0:8] + total[:, 8:16]).reshape(ROWS, 128)

    def raw(n):
        copies = []
        for k in (2, 1, 3):
            y_out[n, k] = raw_chunk(n, k)
            copies.append(
                send(y_out.at[n, k], y_in.at[n, 4 - k], y_s.at[n, k], y_r.at[n, k], to_y(k))
            )
        y_sum[n] = raw_chunk(n, 0)
        return copies

    for copy in og_gather:
        copy.wait_recv()
    make_rhs(0, og_all)
    make_lhs(0, True)
    make_lhs(1, True)

    act_pair.wait_recv()
    pg_t = (own_part + part_in[0]) * slope_v[...]
    pgt_v[...] = pg_t
    pg_v[...] = pg_t.T
    pg_gather = gather(pg_v, pg_all, 1)
    pg_edges = [
        send(pg_v.at[pl.ds(64, 64)], pg_halo.at[pl.ds(0, 64)], halo_s.at[2], halo_r.at[2], to_next),
        send(pg_v.at[pl.ds(0, 64)], pg_halo.at[pl.ds(64, 64)], halo_s.at[3], halo_r.at[3], to_last),
    ]
    pg_all[c, 0] = pg_v[...]

    patch(pg_t, 1)
    loads[4].wait()
    split_weight(1, wb1)
    conv_middle(wb1)

    for copy in edges:
        copy.wait_recv()
    make_lhs(0, False)
    second_y = raw(0)
    make_lhs(1, False)
    for copy in pg_gather:
        copy.wait_recv()
    make_rhs(1, pg_all)
    first_y = raw(1)

    for copy in pg_edges:
        copy.wait_recv()
    patch_edges(pgt_v[...], pg_halo)
    part_out[1] = conv_rest(wb1, 1 - f)
    in_pair = send(part_out.at[1], part_in.at[1], pair_s.at[1], pair_r.at[1], to_filter)
    own_grad = conv_rest(wb1, f)

    for n, copies in ((0, second_y), (1, first_y)):
        for copy in copies:
            copy.wait_recv()
        y_sum[n] = (y_sum[n] + y_in[n, 1]) + (y_in[n, 2] + y_in[n, 3])
        for zz in range(4):
            z_out[zz, n, 0:54, :] = y_sum[n, pl.ds(zz, 54, stride=4), :]
            z_out[zz, n, 54:56, :] = jnp.zeros((2, 128), F32)
    z_copies = [
        send(z_out.at[(zl + k) % 4], z_in.at[4 - k], z_s.at[k], z_r.at[k], to_z(k)) for k in (1, 2, 3)
    ]
    for copy in z_copies:
        copy.wait_recv()
    x_out[...] = ((z_out[zl] + z_in[1]) + (z_in[2] + z_in[3])) * (1.0 / 128.0)
    x_copies = [
        send(x_out, x_all.at[s], x_s.at[k], x_r.at[k], (d, (s + k) % 4, f)) for k in (1, 2, 3)
    ]
    x_all[s] = x_out[...]

    in_pair.wait_recv()
    grad_out[...] = own_grad + part_in[1]

    for copy in x_copies:
        copy.wait_recv()

    for copy in started:
        copy.wait_send()


def finish(grad_t, x_all, grad_out, first_out, second_out):
    grad_out[...] = grad_t[...].T
    for n, out in ((0, second_out), (1, first_out)):
        for x in range(4):
            for e in range(2):
                out[pl.ds(2 * x + e, TAPS, stride=8), :] = x_all[x, n, pl.ds(e, TAPS, stride=2), :]


def local(inputs, pre_gelu, output_grad, first_weight, second_weight):
    shape = inputs.shape
    hbm = pl.BlockSpec(memory_space=pl.ANY)
    vmem = pl.BlockSpec(memory_space=pltpu.VMEM)
    dma = pltpu.SemaphoreType.DMA
    block = (128, 128)
    parts = pl.pallas_call(
        kernel,
        out_shape=(
            jax.ShapeDtypeStruct(block, F32),
            jax.ShapeDtypeStruct((4, 2, 56, 128), F32),
        ),
        in_specs=[hbm] * 5,
        out_specs=(vmem, vmem),
        scratch_shapes=[
            pltpu.VMEM(block, F32),
            pltpu.VMEM(block, F32),
            pltpu.VMEM(block, F32),
            pltpu.VMEM((2, TAPS, 256, 128), F32),
            pltpu.VMEM((2, 256, K_CONV), BF16),
            pltpu.VMEM((2, 256, K_CONV), BF16),
            pltpu.VMEM((K_CONV, 256), BF16),
            pltpu.VMEM((2, 256, 256), F32),
            pltpu.VMEM(block, F32),
            pltpu.VMEM(block, F32),
            pltpu.VMEM(block, F32),
            pltpu.VMEM((2,) + block, F32),
            pltpu.VMEM((2, 4, 2, 16, 128), F32),
            pltpu.VMEM((2, 4, 2, 2, 16, 128), F32),
            pltpu.VMEM((4, 2, 2, 16, 128), F32),
            pltpu.VMEM((4, 2, 2, 16, 128), F32),
            pltpu.VMEM((2, 4) + block, F32),
            pltpu.VMEM((2, 4) + block, F32),
            pltpu.VMEM((2, 1024, 256), BF16),
            pltpu.VMEM((2, 4, TAPS * 16, 1024), BF16),
            pltpu.VMEM((2,) + block, F32),
            pltpu.VMEM((2,) + block, F32),
            pltpu.VMEM(block, F32),
            pltpu.VMEM(block, F32),
            pltpu.VMEM((2, 4, ROWS, 128), F32),
            pltpu.VMEM((2, 4, ROWS, 128), F32),
            pltpu.VMEM((2, ROWS, 128), F32),
            pltpu.VMEM((4, 2, 56, 128), F32),
            pltpu.VMEM((4, 2, 56, 128), F32),
            pltpu.VMEM((2, 56, 128), F32),
            dma((5,)),
            dma((4,)), dma((4,)),
            dma((2,)), dma((2,)),
            dma((2, 7)), dma((2, 7)),
            dma((15,)), dma((15,)),
            dma((2,)), dma((2,)),
            dma((2, 4)), dma((2, 4)),
            dma((4,)), dma((4,)),
            dma((4,)), dma((4,)),
        ],
        compiler_params=pltpu.CompilerParams(
            collective_id=1, has_side_effects=True, vmem_limit_bytes=56 << 20
        ),
        name="backward",
    )(
        inputs.reshape(block),
        pre_gelu.reshape(block),
        output_grad.reshape(block),
        first_weight,
        second_weight,
    )
    grad, first, second = pl.pallas_call(
        finish,
        out_shape=(
            jax.ShapeDtypeStruct(block, F32),
            jax.ShapeDtypeStruct((ROWS, 128), F32),
            jax.ShapeDtypeStruct((ROWS, 128), F32),
        ),
        in_specs=[vmem] * 2,
        out_specs=(vmem, vmem, vmem),
        name="finish",
    )(*parts)
    return grad.reshape(shape), first.reshape(TAPS, 8, 128), second.reshape(TAPS, 8, 128)


def solution(mesh):
    field = P("sample", "depth", None, None, "filter")
    return jax.shard_map(
        local,
        mesh=mesh,
        in_specs=(field, field, field, P(None, None, "filter"), P(None, None, "filter")),
        out_specs=(field, P(None, "depth", "filter"), P(None, "depth", "filter")),
        check_vma=False,
    )
```

```python
import jax
import jax.numpy as jnp
from jax import lax
from jax.experimental import pallas as pl
from jax.experimental.pallas import tpu as pltpu
from jax.sharding import PartitionSpec as P

F32 = jnp.float32
BF16 = jnp.bfloat16
TAPS = 27
ROWS = TAPS * 8
K_CONV = TAPS * 128
THIRD = 9 * 128


def remote(src, dst, send, recv, device):
    return pltpu.make_async_remote_copy(
        src_ref=src,
        dst_ref=dst,
        send_sem=send,
        recv_sem=recv,
        device_id=device,
        device_id_type=pl.DeviceIdType.MESH,
    )


def gelu_pair(pre):
    normal_cdf = 0.5 * (1.0 + lax.erf(pre * 0.7071067811865476))
    density = jnp.exp(-0.5 * pre * pre) * 0.3989422804014327
    return pre * normal_cdf, normal_cdf + pre * density


def parts_of(value):
    high = value.astype(BF16)
    return high, (value - high.astype(F32)).astype(BF16)


def lanes_of(rows):
    return lax.broadcasted_iota(jnp.int32, (rows, 128), 1)


def moved(base, dh, dw):
    if dh == 0 and dw == 0:
        return base
    lane = lanes_of(base.shape[0])
    h = (lane // 8) % 8 + dh
    w = lane % 8 + dw
    inside = (h >= 0) & (h < 8) & (w >= 0) & (w < 8)
    return jnp.where(inside, pltpu.roll(base, (-(dh * 8 + dw)) % 128, 1), 0.0)


def kernel(
    inp_hbm, pre_hbm, og_hbm, w1_hbm, w2_hbm,
    grad_out, x_all,
    og_v, pre_v, inp_v, wf, wb1, wb2, cols, acc,
    og_halo, pg_halo, pair_pre, pair_inp, slope_v, field_t, slices, owned, edge_out, edge_in,
    og_all, pg_all, rhs, lhs, part_out, part_in, pgt_v, pg_v,
    y_out, y_in, y_sum, z_out, z_in, x_out,
    load_sem, halo_s, halo_r, pair_s, pair_r, field_s, field_r, ring_s, ring_r, slice_s, slice_r, edge_s, edge_r,
    y_s, y_r, z_s, z_r, x_s, x_r,
):
    d = lax.axis_index("depth")
    s = lax.axis_index("sample")
    f = lax.axis_index("filter")
    c = d % 2
    chip = d // 2
    zl = chip % 4
    y = d // 8
    partner = d + 1 - 2 * c

    to_filter = (d, s, 1 - f)
    group = [(0, 1)] + [(k, o) for k in (2, 1, 3) for o in (0, 1)]

    def group_device(k, o):
        return (partner if o else d, (s + k) % 4, f)

    to_next, to_last = ((d + 1) % 32, s, f), ((d + 31) % 32, s, f)
    to_next_chip, to_last_chip = ((d + 2) % 32, s, f), ((d + 30) % 32, s, f)

    def to_y(k):
        return ((d + 8 * k) % 32, s, f)

    def to_z(k):
        return (y * 8 + ((zl + k) % 4) * 2 + c, s, f)

    loads = [
        pltpu.make_async_copy(og_hbm, og_v, load_sem.at[0]),
        pltpu.make_async_copy(pre_hbm, pre_v, load_sem.at[1]),
        pltpu.make_async_copy(inp_hbm, inp_v, load_sem.at[2]),
        pltpu.make_async_copy(w2_hbm, wf.at[0], load_sem.at[3]),
        pltpu.make_async_copy(w1_hbm, wf.at[1], load_sem.at[4]),
    ]
    for load in loads:
        load.start()

    barrier = pltpu.get_barrier_semaphore()
    friends = [to_filter, to_next, to_last, to_next_chip, to_last_chip]
    friends += [group_device(k, o) for k, o in group]
    friends += [to_y(k) for k in (1, 2, 3)] + [to_z(k) for k in (1, 2, 3)]
    for friend in friends:
        pl.semaphore_signal(barrier, inc=1, device_id=friend, device_id_type=pl.DeviceIdType.MESH)

    started = []

    def send(*args):
        copy = remote(*args)
        copy.start()
        started.append(copy)
        return copy

    lane = lanes_of(128)
    left = lane < 64

    def patch(base, depth_tap):
        for b in range(3):
            for e in range(3):
                t = 9 * depth_tap + 3 * b + e
                high, low = parts_of(moved(base, 1 - b, 1 - e))
                cols[t * 128 : (t + 1) * 128, 0:128] = high
                cols[t * 128 : (t + 1) * 128, 128:256] = low

    def patch_edges(own, halo_ref):
        edge = halo_ref[...].T
        edge = jnp.where(left & (d == 0), 0.0, edge)
        edge = jnp.where((~left) & (d == 31), 0.0, edge)
        swapped = pltpu.roll(own, 64, 1)
        patch(jnp.where(left, swapped, edge), 0)
        patch(jnp.where(left, edge, swapped), 2)

    def split_weight(n, wb):
        def body(t, carry):
            at = pl.ds(pl.multiple_of(t * 128, 128), 128)
            for h in range(2):
                high, low = parts_of(wf[n, t, h * 128 : (h + 1) * 128, :])
                wb[h, 0:128, at] = high
                wb[h, 128:256, at] = low
            return carry

        lax.fori_loop(0, TAPS, body, 0)

    def product(wb, h, third):
        at = slice(third * THIRD, (third + 1) * THIRD)
        return jnp.dot(wb[h, :, at], cols[at, :], preferred_element_type=F32)

    def fold(total):
        return (total[0:128, 0:128] + total[0:128, 128:256]) + (
            total[128:256, 0:128] + total[128:256, 128:256]
        )

    def conv_middle(wb):
        for h in range(2):
            acc[h] = product(wb, h, 1)

    def conv_rest(wb, h):
        return fold(acc[h] + (product(wb, h, 0) + product(wb, h, 2)))

    def slice_field(n, half):
        for core in range(2):
            for x in range(4):
                for hi in range(2):
                    for e in range(2):
                        row = hi * 8 + e * 4
                        slices[n, core, x, half, row : row + 4, :] = field_t[
                            n, half, pl.ds(64 * hi + 8 * core + 2 * x + e, 4, stride=16), :
                        ]

    loads[0].wait()
    og_t = og_v[...].T
    patch(og_t, 1)
    og_all[c, 0] = og_v[...]
    loads[1].wait()
    act_t, slope_t = gelu_pair(pre_v[...].T)
    slope_v[...] = slope_t
    field_t[0, f] = act_t
    slice_field(0, f)
    loads[2].wait()
    field_t[1, f] = inp_v[...].T
    slice_field(1, f)

    pl.semaphore_wait(barrier, len(friends))

    og_edges = [
        send(og_v.at[pl.ds(64, 64)], og_halo.at[pl.ds(0, 64)], halo_s.at[0], halo_r.at[0], to_next),
        send(og_v.at[pl.ds(0, 64)], og_halo.at[pl.ds(64, 64)], halo_s.at[1], halo_r.at[1], to_last),
    ]
    pre_pair = send(pre_v, pair_pre, field_s.at[0], field_r.at[0], to_filter)

    def gather(src, dst, n):
        copies = [send(src, dst.at[c, 0], ring_s.at[n, 0], ring_r.at[n, 0], group_device(0, 1))]
        for k in (2, 1, 3):
            copies.append(
                send(src, dst.at[c, 4 - k], ring_s.at[n, k], ring_r.at[n, k], group_device(k, 0))
            )
        return copies

    def gather_on(copies, dst, n):
        passed = [copies[0]]
        for k, copy in ((1, copies[2]), (3, copies[3]), (2, copies[1])):
            j = 4 - k
            copy.wait_recv()
            passed.append(
                send(
                    dst.at[c, j], dst.at[c, j], ring_s.at[n, 3 + j], ring_r.at[n, 3 + j], group_device(0, 1)
                )
            )
        return passed

    og_gather = gather(og_v, og_all, 0)

    loads[3].wait()
    split_weight(0, wb2)
    conv_middle(wb2)

    for copy in og_edges:
        copy.wait_recv()
    patch_edges(og_t, og_halo)
    part_out[0] = conv_rest(wb2, 1 - f)
    act_pair = send(part_out.at[0], part_in.at[0], pair_s.at[0], pair_r.at[0], to_filter)
    inp_pair = send(inp_v, pair_inp, field_s.at[1], field_r.at[1], to_filter)
    own_part = conv_rest(wb2, f)

    def send_slices(n, pair, recv):
        pair.wait_recv()
        other = recv[...].T
        if n == 0:
            other, _ = gelu_pair(other)
        field_t[n, 1 - f] = other
        slice_field(n, 1 - f)
        owned[n, c, 0] = slices[n, c, s]
        return [
            send(
                slices.at[n, (1 - c) if o else c, (s + k) % 4],
                owned.at[n, c, (4 - k) % 4],
                slice_s.at[n, i],
                slice_r.at[n, i],
                group_device(k, o),
            )
            for i, (k, o) in enumerate(group)
        ]

    near_edge = lax.broadcasted_iota(jnp.int32, (4, 16, 128), 2) < 64

    def send_edges(n, copies):
        for copy in copies:
            copy.wait_recv()
        above, below = owned[n, 1], owned[n, 0]
        edge_out[n, 0] = jnp.where(near_edge, pltpu.roll(above[:, 0], 64, 2), above[:, 1])
        edge_out[n, 1] = jnp.where(near_edge, below[:, 0], pltpu.roll(below[:, 1], 64, 2))
        return [
            send(edge_out.at[n, i], edge_in.at[n, i], edge_s.at[n, i], edge_r.at[n, i], device)
            for i, device in enumerate((to_next_chip, to_last_chip))
        ]

    def make_rhs(n, ref):
        high, low = parts_of(ref[...].reshape(1024, 128))
        rhs[n, :, 0:128] = high
        rhs[n, :, 128:256] = low

    def make_lhs(n, own_planes):
        near = lanes_of(32) < 64

        def joined(one, two):
            return pltpu.roll(jnp.where(near, two, one), 64, 1)

        def body(k, carry):
            first = owned[n, 0, k].reshape(32, 128)
            last = owned[n, 1, k].reshape(32, 128)
            if own_planes:
                bases = [
                    (first, ((1, 0),)),
                    (joined(first, last), ((2, 0), (0, 1))),
                    (last, ((1, 1),)),
                ]
            else:
                below, above = edge_in[n, 0, k], edge_in[n, 1, k]
                below = jnp.concatenate([pltpu.roll(below, 64, 1), below], axis=0)
                above = jnp.concatenate([above, pltpu.roll(above, 64, 1)], axis=0)
                below = jnp.where(chip == 0, 0.0, below)
                above = jnp.where(chip == 15, 0.0, above)
                bases = [(joined(below, first), ((0, 0),)), (joined(last, above), ((2, 1),))]
            for base, uses in bases:
                for b in range(3):
                    for e in range(3):
                        value = moved(base, b - 1, e - 1)
                        high = value.astype(BF16).astype(F32)
                        low = value - high
                        for yy in range(4):
                            rows = slice(yy * 8, yy * 8 + 8)
                            tile = jnp.concatenate([high[rows], low[rows]], axis=0).astype(BF16)
                            for a, core in uses:
                                t = 9 * a + 3 * b + e
                                at = pl.ds(pl.multiple_of(core * 512 + k * 128, 128), 128)
                                lhs[n, yy, t * 16 : (t + 1) * 16, at] = tile
            return carry

        lax.fori_loop(0, 4, body, 0)

    def raw_chunk(n, k):
        total = jnp.dot(lhs[n, (y + k) % 4], rhs[n], preferred_element_type=F32)
        total = (total[:, 0:128] + total[:, 128:256]).reshape(TAPS, 16, 128)
        return (total[:, 0:8] + total[:, 8:16]).reshape(ROWS, 128)

    def raw(n):
        copies = []
        for k in (2, 1, 3):
            y_out[n, k] = raw_chunk(n, k)
            copies.append(
                send(y_out.at[n, k], y_in.at[n, 4 - k], y_s.at[n, k], y_r.at[n, k], to_y(k))
            )
        y_sum[n] = raw_chunk(n, 0)
        return copies

    loads[4].wait()
    split_weight(1, wb1)
    og_passed = gather_on(og_gather, og_all, 0)
    act_slices = send_slices(0, pre_pair, pair_pre)
    for copy in og_passed:
        copy.wait_recv()
    make_rhs(0, og_all)

    act_pair.wait_recv()
    pg_t = (own_part + part_in[0]) * slope_v[...]
    pgt_v[...] = pg_t
    pg_v[...] = pg_t.T
    pg_gather = gather(pg_v, pg_all, 1)
    pg_edges = [
        send(pg_v.at[pl.ds(64, 64)], pg_halo.at[pl.ds(0, 64)], halo_s.at[2], halo_r.at[2], to_next),
        send(pg_v.at[pl.ds(0, 64)], pg_halo.at[pl.ds(64, 64)], halo_s.at[3], halo_r.at[3], to_last),
    ]
    pg_all[c, 0] = pg_v[...]

    act_edges = send_edges(0, act_slices)
    inp_slices = send_slices(1, inp_pair, pair_inp)
    make_lhs(0, True)
    patch(pg_t, 1)
    conv_middle(wb1)

    for copy in act_edges:
        copy.wait_recv()
    make_lhs(0, False)
    second_y = raw(0)
    inp_edges = send_edges(1, inp_slices)
    make_lhs(1, True)
    pg_passed = gather_on(pg_gather, pg_all, 1)

    for copy in pg_edges:
        copy.wait_recv()
    patch_edges(pgt_v[...], pg_halo)
    part_out[1] = conv_rest(wb1, 1 - f)
    in_pair = send(part_out.at[1], part_in.at[1], pair_s.at[1], pair_r.at[1], to_filter)
    own_grad = conv_rest(wb1, f)

    for copy in inp_edges:
        copy.wait_recv()
    make_lhs(1, False)
    for copy in pg_passed:
        copy.wait_recv()
    make_rhs(1, pg_all)
    first_y = raw(1)

    def sum_y(n, copies):
        for copy in copies:
            copy.wait_recv()
        y_sum[n] = (y_sum[n] + y_in[n, 1]) + (y_in[n, 2] + y_in[n, 3])
        for zz in range(4):
            z_out[n, zz, 0:54, :] = y_sum[n, pl.ds(zz, 54, stride=4), :]
            z_out[n, zz, 54:56, :] = jnp.zeros((2, 128), F32)
        return [
            send(z_out.at[n, (zl + k) % 4], z_in.at[n, 4 - k], z_s.at[n, k], z_r.at[n, k], to_z(k))
            for k in (2, 1, 3)
        ]

    def sum_z(n, copies):
        for copy in copies:
            copy.wait_recv()
        total = (z_out[n, zl] + z_in[n, 1]) + (z_in[n, 2] + z_in[n, 3])
        x_out[n] = total * (1.0 / 128.0)
        x_all[n, s] = x_out[n]
        return [
            send(x_out.at[n], x_all.at[n, s], x_s.at[n, k], x_r.at[n, k], group_device(k, 0))
            for k in (2, 1, 3)
        ]

    second_z = sum_y(0, second_y)
    first_z = sum_y(1, first_y)
    second_x = sum_z(0, second_z)
    in_pair.wait_recv()
    grad_out[...] = own_grad + part_in[1]
    first_x = sum_z(1, first_z)
    for copy in second_x + first_x:
        copy.wait_recv()

    for copy in started:
        copy.wait_send()


def finish(grad_t, x_all, grad_out, first_out, second_out):
    grad_out[...] = grad_t[...].T
    for n, out in ((0, second_out), (1, first_out)):
        for x in range(4):
            for e in range(2):
                out[pl.ds(2 * x + e, TAPS, stride=8), :] = x_all[n, x, pl.ds(e, TAPS, stride=2), :]


def local(inputs, pre_gelu, output_grad, first_weight, second_weight):
    shape = inputs.shape
    hbm = pl.BlockSpec(memory_space=pl.ANY)
    vmem = pl.BlockSpec(memory_space=pltpu.VMEM)
    dma = pltpu.SemaphoreType.DMA
    block = (128, 128)
    parts = pl.pallas_call(
        kernel,
        out_shape=(
            jax.ShapeDtypeStruct(block, F32),
            jax.ShapeDtypeStruct((2, 4, 56, 128), F32),
        ),
        in_specs=[hbm] * 5,
        out_specs=(vmem, vmem),
        scratch_shapes=[
            pltpu.VMEM(block, F32),
            pltpu.VMEM(block, F32),
            pltpu.VMEM(block, F32),
            pltpu.VMEM((2, TAPS, 256, 128), F32),
            pltpu.VMEM((2, 256, K_CONV), BF16),
            pltpu.VMEM((2, 256, K_CONV), BF16),
            pltpu.VMEM((K_CONV, 256), BF16),
            pltpu.VMEM((2, 256, 256), F32),
            pltpu.VMEM(block, F32),
            pltpu.VMEM(block, F32),
            pltpu.VMEM(block, F32),
            pltpu.VMEM(block, F32),
            pltpu.VMEM(block, F32),
            pltpu.VMEM((2, 2) + block, F32),
            pltpu.VMEM((2, 2, 4, 2, 16, 128), F32),
            pltpu.VMEM((2, 2, 4, 2, 16, 128), F32),
            pltpu.VMEM((2, 2, 4, 16, 128), F32),
            pltpu.VMEM((2, 2, 4, 16, 128), F32),
            pltpu.VMEM((2, 4) + block, F32),
            pltpu.VMEM((2, 4) + block, F32),
            pltpu.VMEM((2, 1024, 256), BF16),
            pltpu.VMEM((2, 4, TAPS * 16, 1024), BF16),
            pltpu.VMEM((2,) + block, F32),
            pltpu.VMEM((2,) + block, F32),
            pltpu.VMEM(block, F32),
            pltpu.VMEM(block, F32),
            pltpu.VMEM((2, 4, ROWS, 128), F32),
            pltpu.VMEM((2, 4, ROWS, 128), F32),
            pltpu.VMEM((2, ROWS, 128), F32),
            pltpu.VMEM((2, 4, 56, 128), F32),
            pltpu.VMEM((2, 4, 56, 128), F32),
            pltpu.VMEM((2, 56, 128), F32),
            dma((5,)),
            dma((4,)), dma((4,)),
            dma((2,)), dma((2,)),
            dma((2,)), dma((2,)),
            dma((2, 7)), dma((2, 7)),
            dma((2, 7)), dma((2, 7)),
            dma((2, 2)), dma((2, 2)),
            dma((2, 4)), dma((2, 4)),
            dma((2, 4)), dma((2, 4)),
            dma((2, 4)), dma((2, 4)),
        ],
        compiler_params=pltpu.CompilerParams(
            collective_id=1, has_side_effects=True, vmem_limit_bytes=56 << 20
        ),
        name="backward",
    )(
        inputs.reshape(block),
        pre_gelu.reshape(block),
        output_grad.reshape(block),
        first_weight,
        second_weight,
    )
    grad, first, second = pl.pallas_call(
        finish,
        out_shape=(
            jax.ShapeDtypeStruct(block, F32),
            jax.ShapeDtypeStruct((ROWS, 128), F32),
            jax.ShapeDtypeStruct((ROWS, 128), F32),
        ),
        in_specs=[vmem] * 2,
        out_specs=(vmem, vmem, vmem),
        name="finish",
    )(*parts)
    return grad.reshape(shape), first.reshape(TAPS, 8, 128), second.reshape(TAPS, 8, 128)


def solution(mesh):
    field = P("sample", "depth", None, None, "filter")
    return jax.shard_map(
        local,
        mesh=mesh,
        in_specs=(field, field, field, P(None, None, "filter"), P(None, None, "filter")),
        out_specs=(field, P(None, "depth", "filter"), P(None, "depth", "filter")),
        check_vma=False,
    )
```

```python
import jax
import jax.numpy as jnp
from jax import lax
from jax.experimental import pallas as pl
from jax.experimental.pallas import tpu as pltpu
from jax.sharding import PartitionSpec as P

F32 = jnp.float32
BF16 = jnp.bfloat16
TAPS = 27
ROWS = TAPS * 8
K_CONV = TAPS * 128
THIRD = 9 * 128


def remote(src, dst, send, recv, device):
    return pltpu.make_async_remote_copy(
        src_ref=src,
        dst_ref=dst,
        send_sem=send,
        recv_sem=recv,
        device_id=device,
        device_id_type=pl.DeviceIdType.MESH,
    )


def gelu_pair(pre):
    normal_cdf = 0.5 * (1.0 + lax.erf(pre * 0.7071067811865476))
    density = jnp.exp(-0.5 * pre * pre) * 0.3989422804014327
    return pre * normal_cdf, normal_cdf + pre * density


def parts_of(value):
    high = value.astype(BF16)
    return high, (value - high.astype(F32)).astype(BF16)


def lanes_of(rows):
    return lax.broadcasted_iota(jnp.int32, (rows, 128), 1)


def moved(base, dh, dw):
    if dh == 0 and dw == 0:
        return base
    lane = lanes_of(base.shape[0])
    h = (lane // 8) % 8 + dh
    w = lane % 8 + dw
    inside = (h >= 0) & (h < 8) & (w >= 0) & (w < 8)
    return jnp.where(inside, pltpu.roll(base, (-(dh * 8 + dw)) % 128, 1), 0.0)


def kernel(
    inp_hbm, pre_hbm, og_hbm, w1_hbm, w2_hbm,
    grad_out, x_all,
    og_v, pre_v, inp_v, wf, wb1, wb2, cols, acc,
    og_halo, pg_halo, pair_in, slope_v, field_t, slices, owned, edge_out, edge_in,
    og_all, pg_all, rhs_og, rhs_pg, lhs_act, lhs_inp, part_out, part_in, pgt_v, pg_v,
    y_out, y_in, y_sum, z_out, z_in, x_out,
    load_sem, halo_s, halo_r, pair_s, pair_r, field_s, field_r, ring_s, ring_r, rim_s, rim_r, slice_s, slice_r, edge_s, edge_r,
    y_s, y_r, z_s, z_r, x_s, x_r,
):
    d = lax.axis_index("depth")
    s = lax.axis_index("sample")
    f = lax.axis_index("filter")
    c = d % 2
    chip = d // 2
    zl = chip % 4
    y = d // 8
    partner = d + 1 - 2 * c

    to_filter = (d, s, 1 - f)
    group = [(0, 1)] + [(k, o) for k in (2, 1, 3) for o in (0, 1)]

    def group_device(k, o):
        return (partner if o else d, (s + k) % 4, f)

    to_next, to_last = ((d + 1) % 32, s, f), ((d + 31) % 32, s, f)
    to_next_chip, to_last_chip = ((d + 2) % 32, s, f), ((d + 30) % 32, s, f)

    def to_y(k):
        return ((d + 8 * k) % 32, s, f)

    def to_z(k):
        return (y * 8 + ((zl + k) % 4) * 2 + c, s, f)

    loads = [
        pltpu.make_async_copy(og_hbm, og_v, load_sem.at[0]),
        pltpu.make_async_copy(pre_hbm, pre_v, load_sem.at[1]),
        pltpu.make_async_copy(inp_hbm, inp_v, load_sem.at[2]),
        pltpu.make_async_copy(w2_hbm, wf.at[0], load_sem.at[3]),
        pltpu.make_async_copy(w1_hbm, wf.at[1], load_sem.at[4]),
    ]
    for load in loads:
        load.start()

    barrier = pltpu.get_barrier_semaphore()
    friends = [to_filter, to_next, to_last, to_next_chip, to_last_chip]
    friends += [group_device(k, o) for k, o in group]
    friends += [to_y(k) for k in (1, 2, 3)] + [to_z(k) for k in (1, 2, 3)]
    for friend in friends:
        pl.semaphore_signal(barrier, inc=1, device_id=friend, device_id_type=pl.DeviceIdType.MESH)

    started = []

    def send(*args):
        copy = remote(*args)
        copy.start()
        started.append(copy)
        return copy

    lane = lanes_of(128)
    left = lane < 64

    def patch(base, depth_tap):
        for b in range(3):
            for e in range(3):
                t = 9 * depth_tap + 3 * b + e
                high, low = parts_of(moved(base, 1 - b, 1 - e))
                cols[t * 128 : (t + 1) * 128, 0:128] = high
                cols[t * 128 : (t + 1) * 128, 128:256] = low

    def patch_edges(own, halo_ref):
        edge = halo_ref[...].reshape(128, 128).T
        edge = jnp.where(left & (d == 0), 0.0, edge)
        edge = jnp.where((~left) & (d == 31), 0.0, edge)
        swapped = pltpu.roll(own, 64, 1)
        patch(jnp.where(left, swapped, edge), 0)
        patch(jnp.where(left, edge, swapped), 2)

    def split_weight(n, wb):
        def body(t, carry):
            at = pl.ds(pl.multiple_of(t * 128, 128), 128)
            for h in range(2):
                high, low = parts_of(wf[n, t, h * 128 : (h + 1) * 128, :])
                wb[h, 0:128, at] = high
                wb[h, 128:256, at] = low
            return carry

        lax.fori_loop(0, TAPS, body, 0)

    def product(wb, h, third):
        at = slice(third * THIRD, (third + 1) * THIRD)
        return jnp.dot(wb[h, :, at], cols[at, :], preferred_element_type=F32)

    def fold(total):
        return (total[0:128, 0:128] + total[0:128, 128:256]) + (
            total[128:256, 0:128] + total[128:256, 128:256]
        )

    def conv_middle(wb):
        for h in range(2):
            acc[h] = product(wb, h, 1)

    def conv_rest(wb, h):
        return fold(acc[h] + (product(wb, h, 0) + product(wb, h, 2)))

    def slice_field(n, value):
        field_t[n] = value
        for core in range(2):
            for x in range(4):
                for hi in range(2):
                    for e in range(2):
                        row = hi * 8 + e * 4
                        slices[n, core, x, row : row + 4, :] = field_t[
                            n, pl.ds(64 * hi + 8 * core + 2 * x + e, 4, stride=16), :
                        ]
        owned[n, c, 0, f] = slices[n, c, s]

    loads[0].wait()
    og_t = og_v[...].reshape(128, 128).T
    patch(og_t, 1)
    og_all[0, pl.ds(1 + 2 * c, 2)] = og_v[...]
    loads[1].wait()
    act_t, slope_t = gelu_pair(pre_v[...].T)
    slope_v[...] = slope_t
    slice_field(0, act_t)
    loads[2].wait()
    slice_field(1, inp_v[...].T)

    def clear(k, carry):
        for yy in range(4):
            for t, n in ((0, 0), (18, 2)):
                at = pl.ds(pl.multiple_of(k * 384 + n * 128, 128), 128)
                lhs_act[yy, t * 16 : (t + 9) * 16, at] = jnp.zeros((144, 128), BF16)
        return carry

    lax.fori_loop(0, 4, clear, 0)

    pl.semaphore_wait(barrier, len(friends))

    og_edges = [
        send(og_v.at[1], og_halo.at[0], halo_s.at[0], halo_r.at[0], to_next),
        send(og_v.at[0], og_halo.at[1], halo_s.at[1], halo_r.at[1], to_last),
    ]
    field_pairs = [
        send(slices.at[n], pair_in.at[n], field_s.at[n], field_r.at[n], to_filter) for n in (1, 0)
    ][::-1]

    def send_slices(n, kind, src, half):
        return [
            send(
                src.at[n, (1 - c) if o else c, (s + k) % 4],
                owned.at[n, c, (4 - k) % 4, half],
                slice_s.at[n, kind, i],
                slice_r.at[n, kind, i],
                group_device(k, o),
            )
            for i, (k, o) in enumerate(group)
        ]

    slice_copies = [send_slices(n, 0, slices, f) for n in (1, 0)][::-1]

    def pass_slices(n):
        field_pairs[n].wait_recv()
        owned[n, c, 0, 1 - f] = pair_in[n, c, s]
        slice_copies[n] += send_slices(n, 1, pair_in, 1 - f)


    def gather(src, dst, n):
        copies = [send(src, dst(0), ring_s.at[n, 0], ring_r.at[n, 0], group_device(0, 1))]
        for k in (2, 1, 3):
            copies.append(
                send(src, dst(4 - k), ring_s.at[n, k], ring_r.at[n, k], group_device(k, 0))
            )
        return copies

    def gather_on(copies, dst, n):
        passed = [copies[0]]
        for k, copy in ((1, copies[2]), (3, copies[3]), (2, copies[1])):
            j = 4 - k
            copy.wait_recv()
            passed.append(
                send(
                    dst(j), dst(j), ring_s.at[n, 3 + j], ring_r.at[n, 3 + j], group_device(0, 1)
                )
            )
        return passed

    def og_planes(slot):
        return og_all.at[slot, pl.ds(1 + 2 * c, 2)]

    def pg_planes(slot):
        return pg_all.at[c, slot]

    og_gather = gather(og_v, og_planes, 0)

    loads[3].wait()
    split_weight(0, wb2)
    conv_middle(wb2)

    for copy in og_edges:
        copy.wait_recv()
    patch_edges(og_t, og_halo)
    part_out[0] = conv_rest(wb2, 1 - f)
    act_pair = send(part_out.at[0], part_in.at[0], pair_s.at[0], pair_r.at[0], to_filter)
    own_part = conv_rest(wb2, f)

    near_edge = lax.broadcasted_iota(jnp.int32, (4, 16, 128), 2) < 64

    def send_edges():
        above, below = owned[1, 1], owned[1, 0]
        edge_out[0] = jnp.where(near_edge, pltpu.roll(above[:, 0], 64, 2), above[:, 1])
        edge_out[1] = jnp.where(near_edge, below[:, 0], pltpu.roll(below[:, 1], 64, 2))
        return [
            send(edge_out.at[i], edge_in.at[i], edge_s.at[i], edge_r.at[i], device)
            for i, device in enumerate((to_next_chip, to_last_chip))
        ]

    def make_rhs(rhs, value):
        high, low = parts_of(value)
        rhs[:, 0:128] = high
        rhs[:, 128:256] = low

    near = lanes_of(32) < 64

    def joined(one, two):
        return pltpu.roll(jnp.where(near, two, one), 64, 1)

    def store_shifts(lhs, base, uses):
        for b in range(3):
            for e in range(3):
                value = moved(base, b - 1, e - 1)
                high = value.astype(BF16).astype(F32)
                low = value - high
                for yy in range(4):
                    rows = slice(yy * 8, yy * 8 + 8)
                    tile = jnp.concatenate([high[rows], low[rows]], axis=0).astype(BF16)
                    for a, at in uses:
                        t = 9 * a + 3 * b + e
                        lhs[yy, t * 16 : (t + 1) * 16, at] = tile

    def make_act():
        def body(k, carry):
            at = [pl.ds(pl.multiple_of(k * 384 + n * 128, 128), 128) for n in range(3)]
            first = owned[0, 0, k].reshape(32, 128)
            last = owned[0, 1, k].reshape(32, 128)
            nothing = jnp.zeros((32, 128), F32)
            store_shifts(lhs_act, joined(nothing, first), ((1, at[0]),))
            store_shifts(lhs_act, first, ((2, at[0]), (0, at[1])))
            store_shifts(lhs_act, joined(first, last), ((1, at[1]),))
            store_shifts(lhs_act, last, ((2, at[1]), (0, at[2])))
            store_shifts(lhs_act, joined(last, nothing), ((1, at[2]),))
            return carry

        lax.fori_loop(0, 4, body, 0)

    def make_inp(own_planes):
        def body(k, carry):
            at = [pl.ds(pl.multiple_of(n * 512 + k * 128, 128), 128) for n in range(2)]
            first = owned[1, 0, k].reshape(32, 128)
            last = owned[1, 1, k].reshape(32, 128)
            if own_planes:
                store_shifts(lhs_inp, first, ((1, at[0]),))
                store_shifts(lhs_inp, joined(first, last), ((2, at[0]), (0, at[1])))
                store_shifts(lhs_inp, last, ((1, at[1]),))
            else:
                below, above = edge_in[0, k], edge_in[1, k]
                below = jnp.concatenate([pltpu.roll(below, 64, 1), below], axis=0)
                above = jnp.concatenate([above, pltpu.roll(above, 64, 1)], axis=0)
                below = jnp.where(chip == 0, 0.0, below)
                above = jnp.where(chip == 15, 0.0, above)
                store_shifts(lhs_inp, joined(below, first), ((0, at[0]),))
                store_shifts(lhs_inp, joined(last, above), ((2, at[1]),))
            return carry

        lax.fori_loop(0, 4, body, 0)

    def raw_chunk(n, k):
        lhs, rhs = (lhs_inp, rhs_pg) if n else (lhs_act, rhs_og)
        total = jnp.dot(lhs[(y + k) % 4], rhs[...], preferred_element_type=F32)
        total = (total[:, 0:128] + total[:, 128:256]).reshape(TAPS, 16, 128)
        return (total[:, 0:8] + total[:, 8:16]).reshape(ROWS, 128)

    def raw(n):
        copies = []
        for k in (2, 1, 3):
            y_out[n, k] = raw_chunk(n, k)
            copies.append(
                send(y_out.at[n, k], y_in.at[n, 4 - k], y_s.at[n, k], y_r.at[n, k], to_y(k))
            )
        y_sum[n] = raw_chunk(n, 0)
        return copies

    og_all[0, 5 * c] = og_halo[c]
    rims = [
        send(og_halo.at[c], og_all.at[(4 - k) % 4, 5 * c], rim_s.at[i], rim_r.at[i], group_device(k, o))
        for i, (k, o) in enumerate(group)
    ]
    pass_slices(1)
    og_passed = gather_on(og_gather, og_planes, 0)
    loads[4].wait()
    split_weight(1, wb1)
    pass_slices(0)

    act_pair.wait_recv()
    pg_t = (own_part + part_in[0]) * slope_v[...]
    pgt_v[...] = pg_t
    pg_v[...] = pg_t.T.reshape(2, 64, 128)
    pg_gather = gather(pg_v, pg_planes, 1)
    pg_edges = [
        send(pg_v.at[1], pg_halo.at[0], halo_s.at[2], halo_r.at[2], to_next),
        send(pg_v.at[0], pg_halo.at[1], halo_s.at[3], halo_r.at[3], to_last),
    ]
    pg_all[c, 0] = pg_v[...]

    for copy in slice_copies[1]:
        copy.wait_recv()
    edges = send_edges()
    patch(pg_t, 1)
    conv_middle(wb1)
    make_inp(True)
    for copy in og_passed + rims:
        copy.wait_recv()
    planes = lax.broadcasted_iota(jnp.int32, (4, 6, 64, 128), 1)
    beyond = ((planes == 0) & (chip == 0)) | ((planes == 5) & (chip == 15))
    make_rhs(rhs_og, jnp.where(beyond, 0.0, og_all[...]).reshape(1536, 128))

    for copy in slice_copies[0]:
        copy.wait_recv()
    make_act()
    second_y = raw(0)
    pg_passed = gather_on(pg_gather, pg_planes, 1)
    for copy in edges:
        copy.wait_recv()
    make_inp(False)
    for copy in pg_passed:
        copy.wait_recv()
    make_rhs(rhs_pg, pg_all[...].reshape(1024, 128))
    first_y = raw(1)

    for copy in pg_edges:
        copy.wait_recv()
    patch_edges(pgt_v[...], pg_halo)
    part_out[1] = conv_rest(wb1, 1 - f)
    in_pair = send(part_out.at[1], part_in.at[1], pair_s.at[1], pair_r.at[1], to_filter)
    own_grad = conv_rest(wb1, f)

    def sum_y(n, copies):
        for copy in copies:
            copy.wait_recv()
        y_sum[n] = (y_sum[n] + y_in[n, 1]) + (y_in[n, 2] + y_in[n, 3])
        for zz in range(4):
            z_out[n, zz, 0:54, :] = y_sum[n, pl.ds(zz, 54, stride=4), :]
            z_out[n, zz, 54:56, :] = jnp.zeros((2, 128), F32)
        return [
            send(z_out.at[n, (zl + k) % 4], z_in.at[n, 4 - k], z_s.at[n, k], z_r.at[n, k], to_z(k))
            for k in (2, 1, 3)
        ]

    def sum_z(n, copies):
        for copy in copies:
            copy.wait_recv()
        total = (z_out[n, zl] + z_in[n, 1]) + (z_in[n, 2] + z_in[n, 3])
        x_out[n] = total * (1.0 / 128.0)
        x_all[n, s] = x_out[n]
        return [
            send(x_out.at[n], x_all.at[n, s], x_s.at[n, k], x_r.at[n, k], group_device(k, 0))
            for k in (2, 1, 3)
        ]

    second_z = sum_y(0, second_y)
    first_z = sum_y(1, first_y)
    second_x = sum_z(0, second_z)
    in_pair.wait_recv()
    grad_out[...] = own_grad + part_in[1]
    first_x = sum_z(1, first_z)
    for copy in second_x + first_x:
        copy.wait_recv()

    for copy in started:
        copy.wait_send()


def finish(grad_t, x_all, grad_out, first_out, second_out):
    grad_out[...] = grad_t[...].T
    for n, out in ((0, second_out), (1, first_out)):
        for x in range(4):
            for e in range(2):
                out[pl.ds(2 * x + e, TAPS, stride=8), :] = x_all[n, x, pl.ds(e, TAPS, stride=2), :]


def local(inputs, pre_gelu, output_grad, first_weight, second_weight):
    shape = inputs.shape
    hbm = pl.BlockSpec(memory_space=pl.ANY)
    vmem = pl.BlockSpec(memory_space=pltpu.VMEM)
    dma = pltpu.SemaphoreType.DMA
    block = (128, 128)
    parts = pl.pallas_call(
        kernel,
        out_shape=(
            jax.ShapeDtypeStruct(block, F32),
            jax.ShapeDtypeStruct((2, 4, 56, 128), F32),
        ),
        in_specs=[hbm] * 5,
        out_specs=(vmem, vmem),
        scratch_shapes=[
            pltpu.VMEM((2, 64, 128), F32),
            pltpu.VMEM(block, F32),
            pltpu.VMEM(block, F32),
            pltpu.VMEM((2, TAPS, 256, 128), F32),
            pltpu.VMEM((2, 256, K_CONV), BF16),
            pltpu.VMEM((2, 256, K_CONV), BF16),
            pltpu.VMEM((K_CONV, 256), BF16),
            pltpu.VMEM((2, 256, 256), F32),
            pltpu.VMEM((2, 64, 128), F32),
            pltpu.VMEM((2, 64, 128), F32),
            pltpu.VMEM((2, 2, 4, 16, 128), F32),
            pltpu.VMEM(block, F32),
            pltpu.VMEM((2,) + block, F32),
            pltpu.VMEM((2, 2, 4, 16, 128), F32),
            pltpu.VMEM((2, 2, 4, 2, 16, 128), F32),
            pltpu.VMEM((2, 4, 16, 128), F32),
            pltpu.VMEM((2, 4, 16, 128), F32),
            pltpu.VMEM((4, 6, 64, 128), F32),
            pltpu.VMEM((2, 4, 2, 64, 128), F32),
            pltpu.VMEM((1536, 256), BF16),
            pltpu.VMEM((1024, 256), BF16),
            pltpu.VMEM((4, TAPS * 16, 1536), BF16),
            pltpu.VMEM((4, TAPS * 16, 1024), BF16),
            pltpu.VMEM((2,) + block, F32),
            pltpu.VMEM((2,) + block, F32),
            pltpu.VMEM(block, F32),
            pltpu.VMEM((2, 64, 128), F32),
            pltpu.VMEM((2, 4, ROWS, 128), F32),
            pltpu.VMEM((2, 4, ROWS, 128), F32),
            pltpu.VMEM((2, ROWS, 128), F32),
            pltpu.VMEM((2, 4, 56, 128), F32),
            pltpu.VMEM((2, 4, 56, 128), F32),
            pltpu.VMEM((2, 56, 128), F32),
            dma((5,)),
            dma((4,)), dma((4,)),
            dma((2,)), dma((2,)),
            dma((2,)), dma((2,)),
            dma((2, 7)), dma((2, 7)),
            dma((7,)), dma((7,)),
            dma((2, 2, 7)), dma((2, 2, 7)),
            dma((2,)), dma((2,)),
            dma((2, 4)), dma((2, 4)),
            dma((2, 4)), dma((2, 4)),
            dma((2, 4)), dma((2, 4)),
        ],
        compiler_params=pltpu.CompilerParams(
            collective_id=1, has_side_effects=True, vmem_limit_bytes=56 << 20
        ),
        name="backward",
    )(
        inputs.reshape(block),
        pre_gelu.reshape(block),
        output_grad.reshape(2, 64, 128),
        first_weight,
        second_weight,
    )
    grad, first, second = pl.pallas_call(
        finish,
        out_shape=(
            jax.ShapeDtypeStruct(block, F32),
            jax.ShapeDtypeStruct((ROWS, 128), F32),
            jax.ShapeDtypeStruct((ROWS, 128), F32),
        ),
        in_specs=[vmem] * 2,
        out_specs=(vmem, vmem, vmem),
        name="finish",
    )(*parts)
    return grad.reshape(shape), first.reshape(TAPS, 8, 128), second.reshape(TAPS, 8, 128)


def solution(mesh):
    field = P("sample", "depth", None, None, "filter")
    return jax.shard_map(
        local,
        mesh=mesh,
        in_specs=(field, field, field, P(None, None, "filter"), P(None, None, "filter")),
        out_specs=(field, P(None, "depth", "filter"), P(None, "depth", "filter")),
        check_vma=False,
    )
```

```python
import jax
import jax.numpy as jnp
from jax import lax
from jax.experimental import pallas as pl
from jax.experimental.pallas import tpu as pltpu
from jax.sharding import PartitionSpec as P

F32 = jnp.float32
BF16 = jnp.bfloat16
TAPS = 27
ROWS = TAPS * 8
K_CONV = TAPS * 128
THIRD = 9 * 128


def remote(src, dst, send, recv, device):
    return pltpu.make_async_remote_copy(
        src_ref=src,
        dst_ref=dst,
        send_sem=send,
        recv_sem=recv,
        device_id=device,
        device_id_type=pl.DeviceIdType.MESH,
    )


def gelu_pair(pre):
    normal_cdf = 0.5 * (1.0 + lax.erf(pre * 0.7071067811865476))
    density = jnp.exp(-0.5 * pre * pre) * 0.3989422804014327
    return pre * normal_cdf, normal_cdf + pre * density


def parts_of(value):
    high = value.astype(BF16)
    return high, (value - high.astype(F32)).astype(BF16)


def lanes_of(rows):
    return lax.broadcasted_iota(jnp.int32, (rows, 128), 1)


def moved(base, dh, dw):
    if dh == 0 and dw == 0:
        return base
    lane = lanes_of(base.shape[0])
    h = (lane // 8) % 8 + dh
    w = lane % 8 + dw
    inside = (h >= 0) & (h < 8) & (w >= 0) & (w < 8)
    return jnp.where(inside, pltpu.roll(base, (-(dh * 8 + dw)) % 128, 1), 0.0)


def kernel(
    inp_hbm, pre_hbm, og_hbm, w1_hbm, w2_hbm,
    grad_out, x_all,
    og_v, pre_v, inp_v, wf, wb1, wb2, cols, acc,
    og_halo, pg_halo, pair_in, slope_v, field_t, slices, owned, edge_out, edge_in,
    og_all, pg_all, rhs_og, rhs_pg, lhs_act, lhs_inp, part_out, part_in, pgt_v, pg_v,
    y_out, y_in, y_sum, z_out, z_in, x_out,
    load_sem, halo_s, halo_r, pair_s, pair_r, field_s, field_r, ring_s, ring_r, rim_s, rim_r, slice_s, slice_r, edge_s, edge_r,
    y_s, y_r, z_s, z_r, x_s, x_r,
):
    d = lax.axis_index("depth")
    s = lax.axis_index("sample")
    f = lax.axis_index("filter")
    c = d % 2
    chip = d // 2
    zl = chip % 4
    y = d // 8
    partner = d + 1 - 2 * c

    to_filter = (d, s, 1 - f)
    group = [(0, 1)] + [(k, o) for k in (2, 1, 3) for o in (0, 1)]

    def group_device(k, o):
        return (partner if o else d, (s + k) % 4, f)

    to_next, to_last = ((d + 1) % 32, s, f), ((d + 31) % 32, s, f)
    to_next_chip, to_last_chip = ((d + 2) % 32, s, f), ((d + 30) % 32, s, f)

    def to_y(k):
        return ((d + 8 * k) % 32, s, f)

    def to_z(k):
        return (y * 8 + ((zl + k) % 4) * 2 + c, s, f)

    loads = [
        pltpu.make_async_copy(og_hbm, og_v, load_sem.at[0]),
        pltpu.make_async_copy(pre_hbm, pre_v, load_sem.at[1]),
        pltpu.make_async_copy(inp_hbm, inp_v, load_sem.at[2]),
        pltpu.make_async_copy(w2_hbm, wf.at[0], load_sem.at[3]),
        pltpu.make_async_copy(w1_hbm, wf.at[1], load_sem.at[4]),
    ]
    for load in loads:
        load.start()

    barrier = pltpu.get_barrier_semaphore()
    friends = [to_filter, to_next, to_last, to_next_chip, to_last_chip]
    friends += [group_device(k, o) for k, o in group]
    friends += [to_y(k) for k in (1, 2, 3)] + [to_z(k) for k in (1, 2, 3)]
    for friend in friends:
        pl.semaphore_signal(barrier, inc=1, device_id=friend, device_id_type=pl.DeviceIdType.MESH)

    started = []

    def send(*args):
        copy = remote(*args)
        copy.start()
        started.append(copy)
        return copy

    lane = lanes_of(128)
    left = lane < 64

    def patch(base, depth_tap):
        for b in range(3):
            for e in range(3):
                t = 9 * depth_tap + 3 * b + e
                high, low = parts_of(moved(base, 1 - b, 1 - e))
                cols[t * 128 : (t + 1) * 128, 0:128] = high
                cols[t * 128 : (t + 1) * 128, 128:256] = low

    def patch_edges(own, halo_ref):
        edge = halo_ref[...].reshape(128, 128).T
        edge = jnp.where(left & (d == 0), 0.0, edge)
        edge = jnp.where((~left) & (d == 31), 0.0, edge)
        swapped = pltpu.roll(own, 64, 1)
        patch(jnp.where(left, swapped, edge), 0)
        patch(jnp.where(left, edge, swapped), 2)

    def split_weight(n, wb):
        def body(t, carry):
            at = pl.ds(pl.multiple_of(t * 128, 128), 128)
            for h in range(2):
                high, low = parts_of(wf[n, t, h * 128 : (h + 1) * 128, :])
                wb[h, 0:128, at] = high
                wb[h, 128:256, at] = low
            return carry

        lax.fori_loop(0, TAPS, body, 0)

    def product(wb, h, third):
        at = slice(third * THIRD, (third + 1) * THIRD)
        return jnp.dot(wb[h, :, at], cols[at, :], preferred_element_type=F32)

    def fold(total):
        return (total[0:128, 0:128] + total[0:128, 128:256]) + (
            total[128:256, 0:128] + total[128:256, 128:256]
        )

    def conv_middle(wb):
        for h in range(2):
            acc[h] = product(wb, h, 1)

    def conv_rest(wb, h):
        return fold(acc[h] + (product(wb, h, 0) + product(wb, h, 2)))

    def slice_field(n, value):
        field_t[n] = value
        for core in range(2):
            for x in range(4):
                for hi in range(2):
                    for e in range(2):
                        row = hi * 8 + e * 4
                        slices[n, core, x, row : row + 4, :] = field_t[
                            n, pl.ds(64 * hi + 8 * core + 2 * x + e, 4, stride=16), :
                        ]
        owned[n, c, 0, f] = slices[n, c, s]

    loads[0].wait()
    og_t = og_v[...].reshape(128, 128).T
    patch(og_t, 1)
    og_all[0, pl.ds(1 + 2 * c, 2)] = og_v[...]
    loads[1].wait()
    act_t, slope_t = gelu_pair(pre_v[...].T)
    slope_v[...] = slope_t
    slice_field(0, act_t)
    loads[2].wait()
    slice_field(1, inp_v[...].T)

    def clear(k, carry):
        for yy in range(4):
            for t, n in ((0, 0), (18, 2)):
                at = pl.ds(pl.multiple_of(k * 384 + n * 128, 128), 128)
                lhs_act[yy, t * 16 : (t + 9) * 16, at] = jnp.zeros((144, 128), BF16)
        return carry

    lax.fori_loop(0, 4, clear, 0)

    pl.semaphore_wait(barrier, len(friends))

    og_edges = [
        send(og_v.at[1], og_halo.at[0], halo_s.at[0], halo_r.at[0], to_next),
        send(og_v.at[0], og_halo.at[1], halo_s.at[1], halo_r.at[1], to_last),
    ]
    field_pairs = [
        send(slices.at[n], pair_in.at[n], field_s.at[n], field_r.at[n], to_filter) for n in (1, 0)
    ][::-1]

    def send_slices(n, kind, src, half):
        return [
            send(
                src.at[n, (1 - c) if o else c, (s + k) % 4],
                owned.at[n, c, (4 - k) % 4, half],
                slice_s.at[n, kind, i],
                slice_r.at[n, kind, i],
                group_device(k, o),
            )
            for i, (k, o) in enumerate(group)
        ]

    slice_copies = [send_slices(n, 0, slices, f) for n in (1, 0)][::-1]

    def pass_slices(n):
        field_pairs[n].wait_recv()
        owned[n, c, 0, 1 - f] = pair_in[n, c, s]
        slice_copies[n] += send_slices(n, 1, pair_in, 1 - f)


    def gather(src, dst, n):
        copies = [send(src, dst(0), ring_s.at[n, 0], ring_r.at[n, 0], group_device(0, 1))]
        for k in (2, 1, 3):
            copies.append(
                send(src, dst(4 - k), ring_s.at[n, k], ring_r.at[n, k], group_device(k, 0))
            )
        return copies

    def gather_on(copies, dst, n):
        passed = [copies[0]]
        for k, copy in ((1, copies[2]), (3, copies[3]), (2, copies[1])):
            j = 4 - k
            copy.wait_recv()
            passed.append(
                send(
                    dst(j), dst(j), ring_s.at[n, 3 + j], ring_r.at[n, 3 + j], group_device(0, 1)
                )
            )
        return passed

    def og_planes(slot):
        return og_all.at[slot, pl.ds(1 + 2 * c, 2)]

    def pg_planes(slot):
        return pg_all.at[c, slot]

    og_gather = gather(og_v, og_planes, 0)

    loads[3].wait()
    split_weight(0, wb2)
    conv_middle(wb2)

    for copy in og_edges:
        copy.wait_recv()
    patch_edges(og_t, og_halo)
    part_out[0] = conv_rest(wb2, 1 - f)
    act_pair = send(part_out.at[0], part_in.at[0], pair_s.at[0], pair_r.at[0], to_filter)
    own_part = conv_rest(wb2, f)

    near_edge = lax.broadcasted_iota(jnp.int32, (4, 16, 128), 2) < 64

    def send_edges():
        above, below = owned[1, 1], owned[1, 0]
        edge_out[0] = jnp.where(near_edge, pltpu.roll(above[:, 0], 64, 2), above[:, 1])
        edge_out[1] = jnp.where(near_edge, below[:, 0], pltpu.roll(below[:, 1], 64, 2))
        return [
            send(edge_out.at[i], edge_in.at[i], edge_s.at[i], edge_r.at[i], device)
            for i, device in enumerate((to_next_chip, to_last_chip))
        ]

    def make_rhs(rhs, value):
        high, low = parts_of(value)
        rhs[:, 0:128] = high
        rhs[:, 128:256] = low

    near = lanes_of(32) < 64

    def joined(one, two):
        return pltpu.roll(jnp.where(near, two, one), 64, 1)

    def store_shifts(lhs, base, uses):
        for b in range(3):
            for e in range(3):
                value = moved(base, b - 1, e - 1)
                high = value.astype(BF16).astype(F32)
                low = value - high
                for yy in range(4):
                    rows = slice(yy * 8, yy * 8 + 8)
                    tile = jnp.concatenate([high[rows], low[rows]], axis=0).astype(BF16)
                    for a, at in uses:
                        t = 9 * a + 3 * b + e
                        lhs[yy, t * 16 : (t + 1) * 16, at] = tile

    def make_act():
        def body(k, carry):
            at = [pl.ds(pl.multiple_of(k * 384 + n * 128, 128), 128) for n in range(3)]
            first = owned[0, 0, k].reshape(32, 128)
            last = owned[0, 1, k].reshape(32, 128)
            nothing = jnp.zeros((32, 128), F32)
            store_shifts(lhs_act, joined(nothing, first), ((1, at[0]),))
            store_shifts(lhs_act, first, ((2, at[0]), (0, at[1])))
            store_shifts(lhs_act, joined(first, last), ((1, at[1]),))
            store_shifts(lhs_act, last, ((2, at[1]), (0, at[2])))
            store_shifts(lhs_act, joined(last, nothing), ((1, at[2]),))
            return carry

        lax.fori_loop(0, 4, body, 0)

    def make_inp(own_planes):
        def body(k, carry):
            at = [pl.ds(pl.multiple_of(n * 512 + k * 128, 128), 128) for n in range(2)]
            first = owned[1, 0, k].reshape(32, 128)
            last = owned[1, 1, k].reshape(32, 128)
            if own_planes:
                store_shifts(lhs_inp, first, ((1, at[0]),))
                store_shifts(lhs_inp, joined(first, last), ((2, at[0]), (0, at[1])))
                store_shifts(lhs_inp, last, ((1, at[1]),))
            else:
                below, above = edge_in[0, k], edge_in[1, k]
                below = jnp.concatenate([pltpu.roll(below, 64, 1), below], axis=0)
                above = jnp.concatenate([above, pltpu.roll(above, 64, 1)], axis=0)
                below = jnp.where(chip == 0, 0.0, below)
                above = jnp.where(chip == 15, 0.0, above)
                store_shifts(lhs_inp, joined(below, first), ((0, at[0]),))
                store_shifts(lhs_inp, joined(last, above), ((2, at[1]),))
            return carry

        lax.fori_loop(0, 4, body, 0)

    def raw_chunk(n, k):
        lhs, rhs = (lhs_inp, rhs_pg) if n else (lhs_act, rhs_og)
        total = jnp.dot(lhs[(y + k) % 4], rhs[...], preferred_element_type=F32)
        total = (total[:, 0:128] + total[:, 128:256]).reshape(TAPS, 16, 128)
        return (total[:, 0:8] + total[:, 8:16]).reshape(ROWS, 128)

    def raw(n):
        copies = []
        for k in (2, 1, 3):
            y_out[n, k] = raw_chunk(n, k)
            copies.append(
                send(y_out.at[n, k], y_in.at[n, 4 - k], y_s.at[n, k], y_r.at[n, k], to_y(k))
            )
        y_sum[n] = raw_chunk(n, 0)
        return copies

    og_all[0, 5 * c] = og_halo[c]
    rims = [
        send(og_halo.at[c], og_all.at[(4 - k) % 4, 5 * c], rim_s.at[i], rim_r.at[i], group_device(k, o))
        for i, (k, o) in enumerate(group)
    ]
    pass_slices(1)
    og_passed = gather_on(og_gather, og_planes, 0)
    loads[4].wait()
    split_weight(1, wb1)
    pass_slices(0)

    act_pair.wait_recv()
    pg_t = (own_part + part_in[0]) * slope_v[...]
    pgt_v[...] = pg_t
    pg_v[...] = pg_t.T.reshape(2, 64, 128)
    pg_gather = [
        send(pg_v, pg_planes((4 - k) % 4), ring_s.at[1, i], ring_r.at[1, i], group_device(k, o))
        for i, (k, o) in enumerate(group)
    ]
    pg_edges = [
        send(pg_v.at[1], pg_halo.at[0], halo_s.at[2], halo_r.at[2], to_next),
        send(pg_v.at[0], pg_halo.at[1], halo_s.at[3], halo_r.at[3], to_last),
    ]
    pg_all[c, 0] = pg_v[...]

    for copy in slice_copies[1]:
        copy.wait_recv()
    edges = send_edges()
    patch(pg_t, 1)
    conv_middle(wb1)
    make_inp(True)
    for copy in og_passed + rims:
        copy.wait_recv()
    planes = lax.broadcasted_iota(jnp.int32, (4, 6, 64, 128), 1)
    beyond = ((planes == 0) & (chip == 0)) | ((planes == 5) & (chip == 15))
    make_rhs(rhs_og, jnp.where(beyond, 0.0, og_all[...]).reshape(1536, 128))

    for copy in slice_copies[0]:
        copy.wait_recv()
    make_act()
    second_y = raw(0)
    pg_passed = pg_gather
    for copy in edges:
        copy.wait_recv()
    make_inp(False)
    for copy in pg_passed:
        copy.wait_recv()
    make_rhs(rhs_pg, pg_all[...].reshape(1024, 128))
    first_y = raw(1)

    for copy in pg_edges:
        copy.wait_recv()
    patch_edges(pgt_v[...], pg_halo)
    part_out[1] = conv_rest(wb1, 1 - f)
    in_pair = send(part_out.at[1], part_in.at[1], pair_s.at[1], pair_r.at[1], to_filter)
    own_grad = conv_rest(wb1, f)

    def sum_y(n, copies):
        for copy in copies:
            copy.wait_recv()
        y_sum[n] = (y_sum[n] + y_in[n, 1]) + (y_in[n, 2] + y_in[n, 3])
        for zz in range(4):
            z_out[n, zz, 0:54, :] = y_sum[n, pl.ds(zz, 54, stride=4), :]
            z_out[n, zz, 54:56, :] = jnp.zeros((2, 128), F32)
        return [
            send(z_out.at[n, (zl + k) % 4], z_in.at[n, 4 - k], z_s.at[n, k], z_r.at[n, k], to_z(k))
            for k in (2, 1, 3)
        ]

    def sum_z(n, copies):
        for copy in copies:
            copy.wait_recv()
        total = (z_out[n, zl] + z_in[n, 1]) + (z_in[n, 2] + z_in[n, 3])
        x_out[n] = total * (1.0 / 128.0)
        keep = pltpu.make_async_copy(x_out.at[n], x_all.at[n, s], load_sem.at[n])
        keep.start()
        kept.append(keep)
        return [
            send(x_out.at[n], x_all.at[n, s], x_s.at[n, k], x_r.at[n, k], group_device(k, 0))
            for k in (2, 1, 3)
        ]

    kept = []
    second_z = sum_y(0, second_y)
    first_z = sum_y(1, first_y)
    second_x = sum_z(0, second_z)
    act_pair.wait_send()
    in_pair.wait_recv()
    part_out[0] = own_grad + part_in[1]
    keep = pltpu.make_async_copy(part_out.at[0], grad_out, load_sem.at[2])
    keep.start()
    kept.append(keep)
    first_x = sum_z(1, first_z)
    for copy in second_x + first_x:
        copy.wait_recv()

    for copy in started:
        if copy is not act_pair:
            copy.wait_send()
    for keep in kept:
        keep.wait()


def finish(grad_t, x_all, grad_out, first_out, second_out):
    grad_out[...] = grad_t[...].T
    for n, out in ((0, second_out), (1, first_out)):
        for x in range(4):
            for e in range(2):
                out[pl.ds(2 * x + e, TAPS, stride=8), :] = x_all[n, x, pl.ds(e, TAPS, stride=2), :]


def local(inputs, pre_gelu, output_grad, first_weight, second_weight):
    shape = inputs.shape
    hbm = pl.BlockSpec(memory_space=pl.ANY)
    vmem = pl.BlockSpec(memory_space=pltpu.VMEM)
    dma = pltpu.SemaphoreType.DMA
    block = (128, 128)
    parts = pl.pallas_call(
        kernel,
        out_shape=(
            jax.ShapeDtypeStruct(block, F32),
            jax.ShapeDtypeStruct((2, 4, 56, 128), F32),
        ),
        in_specs=[hbm] * 5,
        out_specs=(hbm, hbm),
        scratch_shapes=[
            pltpu.VMEM((2, 64, 128), F32),
            pltpu.VMEM(block, F32),
            pltpu.VMEM(block, F32),
            pltpu.VMEM((2, TAPS, 256, 128), F32),
            pltpu.VMEM((2, 256, K_CONV), BF16),
            pltpu.VMEM((2, 256, K_CONV), BF16),
            pltpu.VMEM((K_CONV, 256), BF16),
            pltpu.VMEM((2, 256, 256), F32),
            pltpu.VMEM((2, 64, 128), F32),
            pltpu.VMEM((2, 64, 128), F32),
            pltpu.VMEM((2, 2, 4, 16, 128), F32),
            pltpu.VMEM(block, F32),
            pltpu.VMEM((2,) + block, F32),
            pltpu.VMEM((2, 2, 4, 16, 128), F32),
            pltpu.VMEM((2, 2, 4, 2, 16, 128), F32),
            pltpu.VMEM((2, 4, 16, 128), F32),
            pltpu.VMEM((2, 4, 16, 128), F32),
            pltpu.VMEM((4, 6, 64, 128), F32),
            pltpu.VMEM((2, 4, 2, 64, 128), F32),
            pltpu.VMEM((1536, 256), BF16),
            pltpu.VMEM((1024, 256), BF16),
            pltpu.VMEM((4, TAPS * 16, 1536), BF16),
            pltpu.VMEM((4, TAPS * 16, 1024), BF16),
            pltpu.VMEM((2,) + block, F32),
            pltpu.VMEM((2,) + block, F32),
            pltpu.VMEM(block, F32),
            pltpu.VMEM((2, 64, 128), F32),
            pltpu.VMEM((2, 4, ROWS, 128), F32),
            pltpu.VMEM((2, 4, ROWS, 128), F32),
            pltpu.VMEM((2, ROWS, 128), F32),
            pltpu.VMEM((2, 4, 56, 128), F32),
            pltpu.VMEM((2, 4, 56, 128), F32),
            pltpu.VMEM((2, 56, 128), F32),
            dma((5,)),
            dma((4,)), dma((4,)),
            dma((2,)), dma((2,)),
            dma((2,)), dma((2,)),
            dma((2, 7)), dma((2, 7)),
            dma((7,)), dma((7,)),
            dma((2, 2, 7)), dma((2, 2, 7)),
            dma((2,)), dma((2,)),
            dma((2, 4)), dma((2, 4)),
            dma((2, 4)), dma((2, 4)),
            dma((2, 4)), dma((2, 4)),
        ],
        compiler_params=pltpu.CompilerParams(
            collective_id=1, has_side_effects=True, vmem_limit_bytes=56 << 20
        ),
        name="backward",
    )(
        inputs.reshape(block),
        pre_gelu.reshape(block),
        output_grad.reshape(2, 64, 128),
        first_weight,
        second_weight,
    )
    grad, first, second = pl.pallas_call(
        finish,
        out_shape=(
            jax.ShapeDtypeStruct(block, F32),
            jax.ShapeDtypeStruct((ROWS, 128), F32),
            jax.ShapeDtypeStruct((ROWS, 128), F32),
        ),
        in_specs=[vmem] * 2,
        out_specs=(vmem, vmem, vmem),
        name="finish",
    )(*parts)
    return grad.reshape(shape), first.reshape(TAPS, 8, 128), second.reshape(TAPS, 8, 128)


def solution(mesh):
    field = P("sample", "depth", None, None, "filter")
    return jax.shard_map(
        local,
        mesh=mesh,
        in_specs=(field, field, field, P(None, None, "filter"), P(None, None, "filter")),
        out_specs=(field, P(None, "depth", "filter"), P(None, "depth", "filter")),
        check_vma=False,
    )
```

```python
import jax
import jax.numpy as jnp
from jax import lax
from jax.experimental import pallas as pl
from jax.experimental.pallas import tpu as pltpu
from jax.sharding import PartitionSpec as P

F32 = jnp.float32
BF16 = jnp.bfloat16
TAPS = 27
ROWS = TAPS * 8
K_CONV = TAPS * 128
THIRD = 9 * 128


def remote(src, dst, send, recv, device):
    return pltpu.make_async_remote_copy(
        src_ref=src,
        dst_ref=dst,
        send_sem=send,
        recv_sem=recv,
        device_id=device,
        device_id_type=pl.DeviceIdType.MESH,
    )


def gelu_pair(pre):
    normal_cdf = 0.5 * (1.0 + lax.erf(pre * 0.7071067811865476))
    density = jnp.exp(-0.5 * pre * pre) * 0.3989422804014327
    return pre * normal_cdf, normal_cdf + pre * density


def parts_of(value):
    high = value.astype(BF16)
    return high, (value - high.astype(F32)).astype(BF16)


def lanes_of(rows):
    return lax.broadcasted_iota(jnp.int32, (rows, 128), 1)


def moved(base, dh, dw):
    if dh == 0 and dw == 0:
        return base
    lane = lanes_of(base.shape[0])
    h = (lane // 8) % 8 + dh
    w = lane % 8 + dw
    inside = (h >= 0) & (h < 8) & (w >= 0) & (w < 8)
    return jnp.where(inside, pltpu.roll(base, (-(dh * 8 + dw)) % 128, 1), 0.0)


def kernel(
    inp_hbm, pre_hbm, og_hbm, w1_hbm, w2_hbm,
    grad_out, x_all,
    og_v, pre_v, inp_v, wf, wb1, wb2, cols, acc,
    og_halo, pg_halo, pair_in, slope_v, field_t, slices, owned, edge_out, edge_in,
    og_all, pg_all, rhs_og, rhs_pg, lhs_act, lhs_inp, part_out, part_in, pgt_v, pg_v,
    y_out, y_in, y_sum, z_out, z_in, x_out,
    load_sem, halo_s, halo_r, pair_s, pair_r, field_s, field_r, ring_s, ring_r, rim_s, rim_r, slice_s, slice_r, edge_s, edge_r,
    y_s, y_r, z_s, z_r, x_s, x_r,
):
    d = lax.axis_index("depth")
    s = lax.axis_index("sample")
    f = lax.axis_index("filter")
    c = d % 2
    chip = d // 2
    zl = chip % 4
    y = d // 8
    partner = d + 1 - 2 * c

    to_filter = (d, s, 1 - f)
    group = [(0, 1)] + [(k, o) for k in (2, 1, 3) for o in (0, 1)]

    def group_device(k, o):
        return (partner if o else d, (s + k) % 4, f)

    to_next, to_last = ((d + 1) % 32, s, f), ((d + 31) % 32, s, f)
    to_next_chip, to_last_chip = ((d + 2) % 32, s, f), ((d + 30) % 32, s, f)

    def to_y(k):
        return ((d + 8 * k) % 32, s, f)

    def to_z(k):
        return (y * 8 + ((zl + k) % 4) * 2 + c, s, f)

    loads = [
        pltpu.make_async_copy(og_hbm, og_v, load_sem.at[0]),
        pltpu.make_async_copy(pre_hbm, pre_v, load_sem.at[1]),
        pltpu.make_async_copy(inp_hbm, inp_v, load_sem.at[2]),
        pltpu.make_async_copy(w2_hbm, wf.at[0], load_sem.at[3]),
        pltpu.make_async_copy(w1_hbm, wf.at[1], load_sem.at[4]),
    ]
    for load in loads:
        load.start()

    barrier = pltpu.get_barrier_semaphore()
    friends = [to_filter, to_next, to_last, to_next_chip, to_last_chip]
    friends += [group_device(k, o) for k, o in group]
    friends += [to_y(k) for k in (1, 2, 3)] + [to_z(k) for k in (1, 2, 3)]
    for friend in friends:
        pl.semaphore_signal(barrier, inc=1, device_id=friend, device_id_type=pl.DeviceIdType.MESH)

    started = []

    def send(*args):
        copy = remote(*args)
        copy.start()
        started.append(copy)
        return copy

    lane = lanes_of(128)
    left = lane < 64

    def patch(base, depth_tap):
        for b in range(3):
            for e in range(3):
                t = 9 * depth_tap + 3 * b + e
                high, low = parts_of(moved(base, 1 - b, 1 - e))
                cols[t * 128 : (t + 1) * 128, 0:128] = high
                cols[t * 128 : (t + 1) * 128, 128:256] = low

    def patch_edges(own, halo_ref):
        edge = halo_ref[...].reshape(128, 128).T
        edge = jnp.where(left & (d == 0), 0.0, edge)
        edge = jnp.where((~left) & (d == 31), 0.0, edge)
        swapped = pltpu.roll(own, 64, 1)
        patch(jnp.where(left, swapped, edge), 0)
        patch(jnp.where(left, edge, swapped), 2)

    def split_weight(n, wb):
        def body(t, carry):
            at = pl.ds(pl.multiple_of(t * 128, 128), 128)
            for h in range(2):
                high, low = parts_of(wf[n, t, h * 128 : (h + 1) * 128, :])
                wb[h, 0:128, at] = high
                wb[h, 128:256, at] = low
            return carry

        lax.fori_loop(0, TAPS, body, 0)

    def product(wb, h, third):
        at = slice(third * THIRD, (third + 1) * THIRD)
        return jnp.dot(wb[h, :, at], cols[at, :], preferred_element_type=F32)

    def fold(total):
        return (total[0:128, 0:128] + total[0:128, 128:256]) + (
            total[128:256, 0:128] + total[128:256, 128:256]
        )

    def conv_middle(wb):
        for h in range(2):
            acc[h] = product(wb, h, 1)

    def conv_rest(wb, h):
        return fold(acc[h] + (product(wb, h, 0) + product(wb, h, 2)))

    def slice_field(n, value):
        field_t[n] = value
        for core in range(2):
            for x in range(4):
                for hi in range(2):
                    for e in range(2):
                        row = hi * 8 + e * 4
                        slices[n, core, x, row : row + 4, :] = field_t[
                            n, pl.ds(64 * hi + 8 * core + 2 * x + e, 4, stride=16), :
                        ]
        owned[n, c, 0, f] = slices[n, c, s]

    loads[0].wait()
    og_t = og_v[...].reshape(128, 128).T
    patch(og_t, 1)
    og_all[0, pl.ds(1 + 2 * c, 2)] = og_v[...]
    loads[1].wait()
    act_t, slope_t = gelu_pair(pre_v[...].T)
    slope_v[...] = slope_t
    slice_field(0, act_t)
    loads[2].wait()
    slice_field(1, inp_v[...].T)

    def clear(k, carry):
        for yy in range(4):
            for t, n in ((0, 0), (18, 2)):
                at = pl.ds(pl.multiple_of(k * 384 + n * 128, 128), 128)
                lhs_act[yy, t * 16 : (t + 9) * 16, at] = jnp.zeros((144, 128), BF16)
        return carry

    lax.fori_loop(0, 4, clear, 0)

    pl.semaphore_wait(barrier, len(friends))

    og_edges = [
        send(og_v.at[1], og_halo.at[0], halo_s.at[0], halo_r.at[0], to_next),
        send(og_v.at[0], og_halo.at[1], halo_s.at[1], halo_r.at[1], to_last),
    ]
    field_pairs = [
        send(slices.at[n], pair_in.at[n], field_s.at[n], field_r.at[n], to_filter) for n in (1, 0)
    ][::-1]

    def send_slices(n, kind, src, half):
        return [
            send(
                src.at[n, (1 - c) if o else c, (s + k) % 4],
                owned.at[n, c, (4 - k) % 4, half],
                slice_s.at[n, kind, i],
                slice_r.at[n, kind, i],
                group_device(k, o),
            )
            for i, (k, o) in enumerate(group)
        ]

    slice_copies = [send_slices(n, 0, slices, f) for n in (1, 0)][::-1]

    def pass_slices(n):
        field_pairs[n].wait_recv()
        owned[n, c, 0, 1 - f] = pair_in[n, c, s]
        slice_copies[n] += send_slices(n, 1, pair_in, 1 - f)


    def gather(src, dst, n):
        copies = [send(src, dst(0), ring_s.at[n, 0], ring_r.at[n, 0], group_device(0, 1))]
        for k in (2, 1, 3):
            copies.append(
                send(src, dst(4 - k), ring_s.at[n, k], ring_r.at[n, k], group_device(k, 0))
            )
        return copies

    def gather_on(copies, dst, n):
        passed = [copies[0]]
        for k, copy in ((1, copies[2]), (3, copies[3]), (2, copies[1])):
            j = 4 - k
            copy.wait_recv()
            passed.append(
                send(
                    dst(j), dst(j), ring_s.at[n, 3 + j], ring_r.at[n, 3 + j], group_device(0, 1)
                )
            )
        return passed

    def og_planes(slot):
        return og_all.at[slot, pl.ds(1 + 2 * c, 2)]

    def pg_planes(slot):
        return pg_all.at[c, slot]

    og_gather = gather(og_v, og_planes, 0)

    loads[3].wait()
    split_weight(0, wb2)
    conv_middle(wb2)

    for copy in og_edges:
        copy.wait_recv()
    patch_edges(og_t, og_halo)
    part_out[0] = conv_rest(wb2, 1 - f)
    act_pair = send(part_out.at[0], part_in.at[0], pair_s.at[0], pair_r.at[0], to_filter)
    own_part = conv_rest(wb2, f)

    near_edge = lax.broadcasted_iota(jnp.int32, (4, 16, 128), 2) < 64

    def send_edges():
        above, below = owned[1, 1], owned[1, 0]
        edge_out[0] = jnp.where(near_edge, pltpu.roll(above[:, 0], 64, 2), above[:, 1])
        edge_out[1] = jnp.where(near_edge, below[:, 0], pltpu.roll(below[:, 1], 64, 2))
        return [
            send(edge_out.at[i], edge_in.at[i], edge_s.at[i], edge_r.at[i], device)
            for i, device in enumerate((to_next_chip, to_last_chip))
        ]

    def make_rhs(rhs, value):
        high, low = parts_of(value)
        rhs[:, 0:128] = high
        rhs[:, 128:256] = low

    near = lanes_of(32) < 64

    def joined(one, two):
        return pltpu.roll(jnp.where(near, two, one), 64, 1)

    def store_shifts(lhs, base, uses):
        for b in range(3):
            for e in range(3):
                value = moved(base, b - 1, e - 1)
                high = value.astype(BF16).astype(F32)
                low = value - high
                for yy in range(4):
                    rows = slice(yy * 8, yy * 8 + 8)
                    tile = jnp.concatenate([high[rows], low[rows]], axis=0).astype(BF16)
                    for a, at in uses:
                        t = 9 * a + 3 * b + e
                        lhs[yy, t * 16 : (t + 1) * 16, at] = tile

    def make_act():
        def body(k, carry):
            at = [pl.ds(pl.multiple_of(k * 384 + n * 128, 128), 128) for n in range(3)]
            first = owned[0, 0, k].reshape(32, 128)
            last = owned[0, 1, k].reshape(32, 128)
            nothing = jnp.zeros((32, 128), F32)
            store_shifts(lhs_act, joined(nothing, first), ((1, at[0]),))
            store_shifts(lhs_act, first, ((2, at[0]), (0, at[1])))
            store_shifts(lhs_act, joined(first, last), ((1, at[1]),))
            store_shifts(lhs_act, last, ((2, at[1]), (0, at[2])))
            store_shifts(lhs_act, joined(last, nothing), ((1, at[2]),))
            return carry

        lax.fori_loop(0, 4, body, 0)

    def make_inp(own_planes):
        def body(k, carry):
            at = [pl.ds(pl.multiple_of(n * 512 + k * 128, 128), 128) for n in range(2)]
            first = owned[1, 0, k].reshape(32, 128)
            last = owned[1, 1, k].reshape(32, 128)
            if own_planes:
                store_shifts(lhs_inp, first, ((1, at[0]),))
                store_shifts(lhs_inp, joined(first, last), ((2, at[0]), (0, at[1])))
                store_shifts(lhs_inp, last, ((1, at[1]),))
            else:
                below, above = edge_in[0, k], edge_in[1, k]
                below = jnp.concatenate([pltpu.roll(below, 64, 1), below], axis=0)
                above = jnp.concatenate([above, pltpu.roll(above, 64, 1)], axis=0)
                below = jnp.where(chip == 0, 0.0, below)
                above = jnp.where(chip == 15, 0.0, above)
                store_shifts(lhs_inp, joined(below, first), ((0, at[0]),))
                store_shifts(lhs_inp, joined(last, above), ((2, at[1]),))
            return carry

        lax.fori_loop(0, 4, body, 0)

    def raw_chunk(n, k):
        lhs, rhs = (lhs_inp, rhs_pg) if n else (lhs_act, rhs_og)
        total = jnp.dot(lhs[(y + k) % 4], rhs[...], preferred_element_type=F32)
        total = (total[:, 0:128] + total[:, 128:256]).reshape(TAPS, 16, 128)
        return (total[:, 0:8] + total[:, 8:16]).reshape(ROWS, 128)

    def raw(n):
        copies = []
        for k in (2, 1, 3):
            y_out[n, k] = raw_chunk(n, k)
            copies.append(
                send(y_out.at[n, k], y_in.at[n, 4 - k], y_s.at[n, k], y_r.at[n, k], to_y(k))
            )
        y_sum[n] = raw_chunk(n, 0)
        return copies

    og_all[0, 5 * c] = og_halo[c]
    rims = [
        send(og_halo.at[c], og_all.at[(4 - k) % 4, 5 * c], rim_s.at[i], rim_r.at[i], group_device(k, o))
        for i, (k, o) in enumerate(group)
    ]
    pass_slices(1)
    og_passed = gather_on(og_gather, og_planes, 0)
    loads[4].wait()
    split_weight(1, wb1)
    pass_slices(0)

    act_pair.wait_recv()
    pg_t = (own_part + part_in[0]) * slope_v[...]
    pgt_v[...] = pg_t
    pg_v[...] = pg_t.T.reshape(2, 64, 128)
    pg_gather = [
        send(pg_v, pg_planes((4 - k) % 4), ring_s.at[1, i], ring_r.at[1, i], group_device(k, o))
        for i, (k, o) in enumerate(group)
    ]
    pg_edges = [
        send(pg_v.at[1], pg_halo.at[0], halo_s.at[2], halo_r.at[2], to_next),
        send(pg_v.at[0], pg_halo.at[1], halo_s.at[3], halo_r.at[3], to_last),
    ]
    pg_all[c, 0] = pg_v[...]

    for copy in slice_copies[1]:
        copy.wait_recv()
    edges = send_edges()
    patch(pg_t, 1)
    conv_middle(wb1)
    make_inp(True)
    for copy in og_passed + rims:
        copy.wait_recv()
    planes = lax.broadcasted_iota(jnp.int32, (4, 6, 64, 128), 1)
    beyond = ((planes == 0) & (chip == 0)) | ((planes == 5) & (chip == 15))
    make_rhs(rhs_og, jnp.where(beyond, 0.0, og_all[...]).reshape(1536, 128))

    for copy in slice_copies[0]:
        copy.wait_recv()
    make_act()
    second_y = raw(0)
    pg_passed = pg_gather
    for copy in edges:
        copy.wait_recv()
    make_inp(False)
    for copy in pg_passed:
        copy.wait_recv()
    make_rhs(rhs_pg, pg_all[...].reshape(1024, 128))
    first_y = raw(1)

    for copy in pg_edges:
        copy.wait_recv()
    patch_edges(pgt_v[...], pg_halo)
    part_out[1] = conv_rest(wb1, 1 - f)
    in_pair = send(part_out.at[1], part_in.at[1], pair_s.at[1], pair_r.at[1], to_filter)
    own_grad = conv_rest(wb1, f)

    def sum_y(n, copies):
        for copy in copies:
            copy.wait_recv()
        y_sum[n] = (y_sum[n] + y_in[n, 1]) + (y_in[n, 2] + y_in[n, 3])
        for zz in range(4):
            z_out[n, zz, 0:54, :] = y_sum[n, pl.ds(zz, 54, stride=4), :]
            z_out[n, zz, 54:56, :] = jnp.zeros((2, 128), F32)
        return [
            send(z_out.at[n, (zl + k) % 4], z_in.at[n, 4 - k], z_s.at[n, k], z_r.at[n, k], to_z(k))
            for k in (2, 1, 3)
        ]

    def sum_z(n, copies):
        for copy in copies:
            copy.wait_recv()
        total = (z_out[n, zl] + z_in[n, 1]) + (z_in[n, 2] + z_in[n, 3])
        x_out[n] = total * (1.0 / 128.0)
        keep = pltpu.make_async_copy(x_out.at[n], x_all.at[n, s], load_sem.at[n])
        keep.start()
        kept.append(keep)
        return [
            send(x_out.at[n], x_all.at[n, s], x_s.at[n, k], x_r.at[n, k], group_device(k, 0))
            for k in (2, 1, 3)
        ]

    kept = []
    second_z = sum_y(0, second_y)
    first_z = sum_y(1, first_y)
    second_x = sum_z(0, second_z)
    act_pair.wait_send()
    in_pair.wait_recv()
    part_out[0] = (own_grad + part_in[1]).T
    keep = pltpu.make_async_copy(part_out.at[0], grad_out, load_sem.at[2])
    keep.start()
    kept.append(keep)
    first_x = sum_z(1, first_z)
    for copy in second_x + first_x:
        copy.wait_recv()

    for copy in started:
        if copy is not act_pair:
            copy.wait_send()
    for keep in kept:
        keep.wait()


def finish(grad_t, x_all, grad_out, first_out, second_out):
    grad_out[...] = grad_t[...]
    for n, out in ((0, second_out), (1, first_out)):
        for x in range(4):
            for e in range(2):
                out[pl.ds(2 * x + e, TAPS, stride=8), :] = x_all[n, x, pl.ds(e, TAPS, stride=2), :]


def local(inputs, pre_gelu, output_grad, first_weight, second_weight):
    shape = inputs.shape
    hbm = pl.BlockSpec(memory_space=pl.ANY)
    vmem = pl.BlockSpec(memory_space=pltpu.VMEM)
    dma = pltpu.SemaphoreType.DMA
    block = (128, 128)
    parts = pl.pallas_call(
        kernel,
        out_shape=(
            jax.ShapeDtypeStruct(block, F32),
            jax.ShapeDtypeStruct((2, 4, 56, 128), F32),
        ),
        in_specs=[hbm] * 5,
        out_specs=(hbm, hbm),
        scratch_shapes=[
            pltpu.VMEM((2, 64, 128), F32),
            pltpu.VMEM(block, F32),
            pltpu.VMEM(block, F32),
            pltpu.VMEM((2, TAPS, 256, 128), F32),
            pltpu.VMEM((2, 256, K_CONV), BF16),
            pltpu.VMEM((2, 256, K_CONV), BF16),
            pltpu.VMEM((K_CONV, 256), BF16),
            pltpu.VMEM((2, 256, 256), F32),
            pltpu.VMEM((2, 64, 128), F32),
            pltpu.VMEM((2, 64, 128), F32),
            pltpu.VMEM((2, 2, 4, 16, 128), F32),
            pltpu.VMEM(block, F32),
            pltpu.VMEM((2,) + block, F32),
            pltpu.VMEM((2, 2, 4, 16, 128), F32),
            pltpu.VMEM((2, 2, 4, 2, 16, 128), F32),
            pltpu.VMEM((2, 4, 16, 128), F32),
            pltpu.VMEM((2, 4, 16, 128), F32),
            pltpu.VMEM((4, 6, 64, 128), F32),
            pltpu.VMEM((2, 4, 2, 64, 128), F32),
            pltpu.VMEM((1536, 256), BF16),
            pltpu.VMEM((1024, 256), BF16),
            pltpu.VMEM((4, TAPS * 16, 1536), BF16),
            pltpu.VMEM((4, TAPS * 16, 1024), BF16),
            pltpu.VMEM((2,) + block, F32),
            pltpu.VMEM((2,) + block, F32),
            pltpu.VMEM(block, F32),
            pltpu.VMEM((2, 64, 128), F32),
            pltpu.VMEM((2, 4, ROWS, 128), F32),
            pltpu.VMEM((2, 4, ROWS, 128), F32),
            pltpu.VMEM((2, ROWS, 128), F32),
            pltpu.VMEM((2, 4, 56, 128), F32),
            pltpu.VMEM((2, 4, 56, 128), F32),
            pltpu.VMEM((2, 56, 128), F32),
            dma((5,)),
            dma((4,)), dma((4,)),
            dma((2,)), dma((2,)),
            dma((2,)), dma((2,)),
            dma((2, 7)), dma((2, 7)),
            dma((7,)), dma((7,)),
            dma((2, 2, 7)), dma((2, 2, 7)),
            dma((2,)), dma((2,)),
            dma((2, 4)), dma((2, 4)),
            dma((2, 4)), dma((2, 4)),
            dma((2, 4)), dma((2, 4)),
        ],
        compiler_params=pltpu.CompilerParams(
            collective_id=1, has_side_effects=True, vmem_limit_bytes=56 << 20
        ),
        name="backward",
    )(
        inputs.reshape(block),
        pre_gelu.reshape(block),
        output_grad.reshape(2, 64, 128),
        first_weight,
        second_weight,
    )
    grad, first, second = pl.pallas_call(
        finish,
        out_shape=(
            jax.ShapeDtypeStruct(block, F32),
            jax.ShapeDtypeStruct((ROWS, 128), F32),
            jax.ShapeDtypeStruct((ROWS, 128), F32),
        ),
        in_specs=[vmem] * 2,
        out_specs=(vmem, vmem, vmem),
        name="finish",
    )(*parts)
    return grad.reshape(shape), first.reshape(TAPS, 8, 128), second.reshape(TAPS, 8, 128)


def solution(mesh):
    field = P("sample", "depth", None, None, "filter")
    return jax.shard_map(
        local,
        mesh=mesh,
        in_specs=(field, field, field, P(None, None, "filter"), P(None, None, "filter")),
        out_specs=(field, P(None, "depth", "filter"), P(None, "depth", "filter")),
        check_vma=False,
    )
```
